32 devices in a mesh: dx: 4 (over z), dy: 4 (over y, x), dz: 2 (over core).
Axes of the slice: x: 2, y: 2, z: 4, core: 2. Of those that a mesh axis runs over, the one named last changes fastest.
Arguments:
- node_state: bfloat16 [8, 8, 4, 32, 128], P('dx', 'dy', 'dz'), may hold values from -6 to 6
- mesh_base: int32 [3, 8, 8, 4, 32], P(None, 'dx', 'dy', 'dz'), may hold values from 0 to 127, as said below
- mesh_frac: float32 [3, 8, 8, 4, 32], P(None, 'dx', 'dy', 'dz'), may hold values from 0 to 1
- charge: float32 [8, 8, 4, 32], P('dx', 'dy', 'dz'), may hold values from -0.5 to 0.5
- nbr_code: int32 [8, 8, 4, 32, 128], P('dx', 'dy', 'dz'), may hold values from 0 to 863, as said below
- nbr_count: int32 [8, 8, 4, 32], P('dx', 'dy', 'dz'), may hold values from 32 to 128, as said below
- radial_weight: float32 [8, 128], replicated, may hold values from -2 to 2
- mix_weight: bfloat16 [3, 128, 128], replicated, may hold values from -0.5 to 0.5
- force_weight: float32 [128], replicated, may hold values from -0.5 to 0.5
Outputs:
- node_next: bfloat16 [8, 8, 4, 32, 128], P('dx', 'dy', 'dz')
- forces: float32 [3, 8, 8, 4, 32], P(None, 'dx', 'dy', 'dz')
The draws below stay inside these ranges and needn't reach their ends.
Inputs may be any that keep to these rules, and one draw needn't show every extreme that they name: `mesh_base`: entry d of an atom in octant (X, Y, Z) lies in the atom's octant: from 32 / 2 times its octant index along d up to 16 more, exclusive. In every octant the first atom sits at the lower end and the second at the upper end in every dimension. `nbr_code`: The first atom of every octant has the largest code in its first slot and 0 in its second. `nbr_count`: slots from the count on are padding. The first atom of every octant has 128 live slots, the second 128 // 4.
All inputs are finite; a program needn't handle non-finite values.
Results may differ from the reference program's by a relative error of at most 0.00095.
The reference program's roundings to bfloat16 on the way (of `edge_values` and `message`) count: a program that leaves them out, or rounds other values in their place, can miss the bound.
Values may be sent and summed in bfloat16 or wider, within the bound.
No kernel may reach another device: no remote copies, remote signals or barrier semaphores. Data moves between devices by JAX's collectives and lax.ppermute only.
A program may use at most 64 MiB of HBM per device.

```python
import math
import jax
import jax.numpy as jnp
from jax import lax

C = 128
NB = 8
NBR = 128
OCT = 32
MB = 32
KZW = 8
MX = 128
MY = 128
MZ = 64
N_DX = 4
N_DY = 4
N_DZ = 2


def draw_mesh_base(key, part):
    half_block = MB // 2
    full_shape = (3, 2 * N_DX, 2 * N_DY, 2 * N_DZ, OCT)
    inside = jax.random.randint(jax.random.fold_in(key, 11), full_shape, 0, half_block, dtype=jnp.int32)
    inside = inside.at[:, :, :, :, 0].set(0)
    inside = inside.at[:, :, :, :, 1].set(half_block - 1)
    octant_x = jnp.broadcast_to(jnp.arange(2 * N_DX, dtype=jnp.int32)[:, None, None, None], full_shape[1:])
    octant_y = jnp.broadcast_to(jnp.arange(2 * N_DY, dtype=jnp.int32)[None, :, None, None], full_shape[1:])
    octant_z = jnp.broadcast_to(jnp.arange(2 * N_DZ, dtype=jnp.int32)[None, None, :, None], full_shape[1:])
    octant = jnp.stack([octant_x, octant_y, octant_z])
    return octant * half_block + inside


def draw_nbr_code(key, part):
    full_shape = (2 * N_DX, 2 * N_DY, 2 * N_DZ, OCT, NBR)
    side_code = jax.random.randint(jax.random.fold_in(key, 13), full_shape, 0, 27, dtype=jnp.int32)
    slot_code = jax.random.randint(jax.random.fold_in(key, 17), full_shape, 0, OCT, dtype=jnp.int32)
    own_slot = jnp.arange(OCT, dtype=jnp.int32)[:, None]
    clashes = (side_code == 13) & (slot_code == own_slot)
    slot_code = jnp.where(clashes, (slot_code + 1) % OCT, slot_code)
    code_rows = side_code * OCT + slot_code
    code_rows = code_rows.at[:, :, :, 0, 0].set(27 * OCT - 1)
    return code_rows.at[:, :, :, 0, 1].set(0)


def draw_nbr_count(key, part):
    full_shape = (2 * N_DX, 2 * N_DY, 2 * N_DZ, OCT)
    counts = jax.random.randint(jax.random.fold_in(key, 19), full_shape, NBR // 4, NBR + 1, dtype=jnp.int32)
    counts = counts.at[:, :, :, 0].set(NBR)
    return counts.at[:, :, :, 1].set(NBR // 4)


def block_levels(own_key, shape, pieces, least, largest):
    loudness, own = 1.0, jax.random.fold_in(own_key, 6)
    for axis_at, parts in pieces:
        draws = jnp.exp(jax.random.uniform(jax.random.fold_in(own, axis_at), (parts,), jnp.float32, least / len(pieces), largest / len(pieces)))
        loudness = loudness * jnp.repeat(draws, shape[axis_at] // parts).reshape([-1 if axis == axis_at else 1 for axis in range(len(shape))])
    return loudness


def centred(stream_key, shape, spread, limit, cuts=(), held_as=jnp.bfloat16):
    drawn = spread * jax.random.normal(stream_key, shape, jnp.float32)
    if cuts:
        drawn = drawn * block_levels(stream_key, shape, cuts, -0.22, 0.18)
    return jnp.clip(drawn, -limit, limit).astype(held_as)


def setup_inputs(seed: int = 0) -> dict:
    key_of = jax.random.split(jax.random.key(seed), 10)
    return {
        "node_state": centred(key_of[0], (2 * N_DX, 2 * N_DY, 2 * N_DZ, OCT, C), 1.0, 6.0, ((0, 4), (1, 4), (2, 2))),
        "mesh_base": draw_mesh_base(jax.random.fold_in(key_of[9], 71), 0),
        "mesh_frac": jnp.clip(1.0 * jax.random.uniform(key_of[2], (3, 2 * N_DX, 2 * N_DY, 2 * N_DZ, OCT), jnp.float32) ** block_levels(key_of[2], (3, 2 * N_DX, 2 * N_DY, 2 * N_DZ, OCT), ((1, 4), (2, 4), (3, 2)), -0.2, 0.2), 0.0, 1.0),
        "charge": jnp.clip(jax.random.uniform(key_of[3], (2 * N_DX, 2 * N_DY, 2 * N_DZ, OCT), jnp.float32, -0.5, 0.5) * block_levels(key_of[3], (2 * N_DX, 2 * N_DY, 2 * N_DZ, OCT), ((0, 4), (1, 4), (2, 2)), -0.4, 0.0), -0.5, 0.5),
        "nbr_code": draw_nbr_code(jax.random.fold_in(key_of[9], 71), 0),
        "nbr_count": draw_nbr_count(jax.random.fold_in(key_of[9], 71), 0),
        "radial_weight": centred(key_of[6], (NB, C), NB ** -0.5, 2.0, (), jnp.float32),
        "mix_weight": centred(key_of[7], (3, C, C), C ** -0.5, 0.5),
        "force_weight": centred(key_of[8], (C,), C ** -0.5, 0.5, (), jnp.float32),
    }


cell_size = 1.13
ewald_beta = 0.625
coulomb = 332.0637
sigma_low = 8.0
sigma_rate = 1.5
highest = lax.Precision.HIGHEST

def spline_terms(fraction):
    remainder = 1.0 - fraction
    frac_square = fraction * fraction
    frac_cube = frac_square * fraction
    weights = jnp.stack([remainder * remainder * remainder / 6.0, (3.0 * frac_cube - 6.0 * frac_square + 4.0) / 6.0, (-3.0 * frac_cube + 3.0 * frac_square + 3.0 * fraction + 1.0) / 6.0, frac_cube / 6.0])
    slopes = jnp.stack([-0.5 * remainder * remainder, 1.5 * frac_square - 2.0 * fraction, -1.5 * frac_square + fraction + 0.5, 0.5 * frac_square])
    return (weights, slopes)

def harmonics(direction):
    unit_x, unit_y, unit_z = (direction[0], direction[1], direction[2])
    root_three = math.sqrt(3.0)
    root_fifteen = math.sqrt(15.0)
    root_five = math.sqrt(5.0)
    return jnp.stack([jnp.ones_like(unit_x), root_three * unit_x, root_three * unit_y, root_three * unit_z, root_fifteen * unit_x * unit_y, root_fifteen * unit_y * unit_z, 0.5 * root_five * (3.0 * unit_z * unit_z - 1.0), root_fifteen * unit_x * unit_z, 0.5 * root_fifteen * (unit_x * unit_x - unit_y * unit_y)])

def edge_terms(displace, active):
    square = lax.optimization_barrier(jnp.sum(displace * displace, axis=0))
    direction = displace / jnp.sqrt(square + 1.0)
    angular = harmonics(direction)
    distance = cell_size * jnp.sqrt(square)
    widths = sigma_low * jnp.power(sigma_rate, jnp.arange(NB).astype(jnp.float32))
    radial = jnp.exp(-jnp.square(distance[None] / widths[:, None, None]))
    products = radial[:, None] * angular[None] * active.astype(jnp.float32)[None, None]
    atom_rows = displace.shape[1]
    return jnp.transpose(products, (2, 0, 1, 3)).reshape(atom_rows, NB * 9, -1).astype(jnp.bfloat16)

def node_update(edge_values, neighbour_state, own_state, radial_weight, mix_weight, force_weight):
    summed = jnp.einsum('bkn,bnc->bkc', edge_values.astype(jnp.float32), neighbour_state.astype(jnp.float32))
    atom_rows = summed.shape[0]
    summed = summed.reshape(atom_rows, NB, 9, -1)
    message = (lax.optimization_barrier(jnp.sum(summed * radial_weight[None, :, None, :], axis=1)) / math.sqrt(NBR)).astype(jnp.bfloat16)
    scalar = jnp.dot(message[:, 0], mix_weight[0], preferred_element_type=jnp.float32)
    vector = jnp.einsum('bmc,cd->bmd', message[:, 1:4].astype(jnp.float32), mix_weight[1].astype(jnp.float32))
    tensor = jnp.einsum('bmc,cd->bmd', message[:, 4:9].astype(jnp.float32), mix_weight[2].astype(jnp.float32))
    invariant = scalar + lax.optimization_barrier(jnp.sum(tensor * tensor, axis=1))
    gating = jax.nn.sigmoid(invariant)
    updated = (own_state.astype(jnp.float32) + jax.nn.silu(invariant)).astype(jnp.bfloat16)
    short_push = lax.optimization_barrier(jnp.sum(vector * (gating * force_weight)[:, None, :], axis=2))
    return (updated, jnp.transpose(short_push))

def phases(wavenumber, cell_index, extent):
    return 2.0 * math.pi / extent * jnp.mod(wavenumber * cell_index, extent).astype(jnp.float32)

def wave_sums(coeff, start_cells, wavenumber, extent, orient):
    wave_re = jnp.zeros((start_cells.shape[0], wavenumber.shape[0]), jnp.float32)
    wave_im = jnp.zeros((start_cells.shape[0], wavenumber.shape[0]), jnp.float32)
    for stencil in range(4):
        angles = phases(wavenumber[None, :], (start_cells + stencil)[:, None], extent)
        wave_re = wave_re + coeff[stencil][:, None] * jnp.cos(angles)
        wave_im = wave_im + coeff[stencil][:, None] * jnp.sin(angles)
    return (wave_re, orient * wave_im)

def cell_table(coeff, local_cells, cell_index):
    table = jnp.zeros((local_cells.shape[0], cell_index.shape[0]), jnp.float32)
    for stencil in range(4):
        match = (cell_index[None, :] == (local_cells + stencil)[:, None]).astype(jnp.float32)
        table = table + coeff[stencil][:, None] * match
    return table

def influence(modes_x, modes_y, modes_z, length_x, length_y, length_z):

    def folded(wavenumber, extent):
        return jnp.where(2 * wavenumber >= extent, wavenumber - extent, wavenumber).astype(jnp.float32) / (cell_size * extent)
    wave_square = jnp.square(folded(modes_x, length_x)) + jnp.square(folded(modes_y, length_y)) + jnp.square(folded(modes_z, length_z))
    volume = cell_size ** 3 * length_x * length_y * length_z
    return coulomb / (math.pi * volume) * jnp.exp(-math.pi ** 2 * wave_square / ewald_beta ** 2) / wave_square

def projected(value_re, value_im, wave_y_re, wave_y_im, wave_z_re, wave_z_im):
    inner_re = lax.optimization_barrier(jnp.sum(value_re * wave_y_re[:, :, None] - value_im * wave_y_im[:, :, None], axis=1))
    inner_im = lax.optimization_barrier(jnp.sum(value_re * wave_y_im[:, :, None] + value_im * wave_y_re[:, :, None], axis=1))
    return 2.0 * lax.optimization_barrier(jnp.sum(inner_re * wave_z_re - inner_im * wave_z_im, axis=1))

def short_range(node_state, places, nbr_code, nbr_count, radial_weight, mix_weight, force_weight):
    wide_x = 2 * N_DX
    wide_y = 2 * N_DY
    wide_z = 2 * N_DZ
    half_block = MB // 2
    columns = wide_x * wide_y
    block_rows = wide_z * OCT
    flat_state = node_state.reshape(-1, C)
    flat_places = places.reshape(3, -1)
    code_table = nbr_code.reshape(columns, block_rows, NBR)
    count_table = nbr_count.reshape(columns, block_rows)
    state_table = node_state.reshape(columns, block_rows, C)
    z_octant = jnp.arange(block_rows, dtype=jnp.int32) // OCT
    slot_index = jnp.arange(NBR, dtype=jnp.int32)

    def one_column(column):
        code_rows = code_table[column]
        count_rows = count_table[column]
        side_code = code_rows // OCT
        slot_code = code_rows % OCT
        reach_x = column // wide_y + side_code // 9 - 1
        reach_y = column % wide_y + side_code // 3 % 3 - 1
        reach_z = z_octant[:, None] + side_code % 3 - 1
        wrapped_x = jnp.mod(reach_x, wide_x)
        wrapped_y = jnp.mod(reach_y, wide_y)
        wrapped_z = jnp.mod(reach_z, wide_z)
        wrap_shift = jnp.stack([(reach_x - wrapped_x) * half_block, (reach_y - wrapped_y) * half_block, (reach_z - wrapped_z) * half_block]).astype(jnp.float32)
        neighbour = ((wrapped_x * wide_y + wrapped_y) * wide_z + wrapped_z) * OCT + slot_code
        own_index = column * block_rows + jnp.arange(block_rows, dtype=jnp.int32)
        own_places = flat_places[:, own_index]
        displace = flat_places[:, neighbour] + wrap_shift - own_places[:, :, None]
        active = slot_index[None, :] < count_rows[:, None]
        edge_values = edge_terms(displace, active)
        return node_update(edge_values, flat_state[neighbour], state_table[column], radial_weight, mix_weight, force_weight)
    return lax.map(one_column, jnp.arange(columns, dtype=jnp.int32))

def long_range(mesh_base, mesh_frac, charge):
    half_block = MB // 2
    span_x = half_block + 3
    wide_y = 2 * N_DY
    columns = 2 * N_DX * wide_y
    block_rows = 2 * N_DZ * OCT
    flat_base = mesh_base.reshape(3, columns, block_rows)
    flat_frac = mesh_frac.reshape(3, columns, block_rows)
    flat_charge = charge.reshape(columns, block_rows)
    mode_count = MY * KZW
    modes_y = jnp.arange(MY, dtype=jnp.int32)
    planes = 1 + jnp.arange(KZW, dtype=jnp.int32)
    span_cells = jnp.arange(span_x, dtype=jnp.int32)

    def column_setup(column):
        base_now = flat_base[:, column]
        weights, slopes = spline_terms(flat_frac[:, column])
        first_x = column // wide_y * half_block
        local_x = base_now[0] - first_x
        return (base_now, weights, slopes, first_x, local_x)

    def forward(carried, column):
        base_now, weights, slopes, first_x, local_x = column_setup(column)
        charges_now = flat_charge[column]
        table_x = cell_table(weights[:, 0], local_x, span_cells)
        wave_y_re, wave_y_im = wave_sums(weights[:, 1], base_now[1], modes_y, MY, -1.0)
        wave_z_re, wave_z_im = wave_sums(weights[:, 2], base_now[2], planes, MZ, -1.0)
        mixed_re = (wave_y_re[:, :, None] * wave_z_re[:, None, :] - wave_y_im[:, :, None] * wave_z_im[:, None, :]).reshape(-1, mode_count)
        mixed_im = (wave_y_re[:, :, None] * wave_z_im[:, None, :] + wave_y_im[:, :, None] * wave_z_re[:, None, :]).reshape(-1, mode_count)
        left_side = jnp.transpose(table_x * charges_now[:, None])
        part_re = jnp.dot(left_side, mixed_re, precision=highest)
        part_im = jnp.dot(left_side, mixed_im, precision=highest)
        row_ids = jnp.mod(first_x + span_cells, MX)
        slab_re, slab_im = carried
        return ((slab_re.at[row_ids].add(part_re), slab_im.at[row_ids].add(part_im)), None)
    initial = (jnp.zeros((MX, mode_count), jnp.float32), jnp.zeros((MX, mode_count), jnp.float32))
    (slab_re, slab_im), _ = lax.scan(forward, initial, jnp.arange(columns, dtype=jnp.int32))
    modes_x = jnp.arange(MX, dtype=jnp.int32)
    angle_x = phases(modes_x[:, None], modes_x[None, :], MX)
    cos_x = jnp.cos(angle_x)
    sin_x = jnp.sin(angle_x)
    spec_re = jnp.dot(cos_x.T, slab_re, precision=highest) + jnp.dot(sin_x.T, slab_im, precision=highest)
    spec_im = jnp.dot(cos_x.T, slab_im, precision=highest) - jnp.dot(sin_x.T, slab_re, precision=highest)
    green_table = influence(modes_x[:, None, None], modes_y[None, :, None], planes[None, None, :], MX, MY, MZ).reshape(MX, mode_count)
    scaled_re = green_table * spec_re
    scaled_im = green_table * spec_im
    back_re = jnp.dot(cos_x, scaled_re, precision=highest) - jnp.dot(sin_x, scaled_im, precision=highest)
    back_im = jnp.dot(sin_x, scaled_re, precision=highest) + jnp.dot(cos_x, scaled_im, precision=highest)

    def backward(column):
        base_now, weights, slopes, first_x, local_x = column_setup(column)
        charges_now = flat_charge[column]
        row_ids = jnp.mod(first_x + span_cells, MX)
        near_re = back_re[row_ids]
        near_im = back_im[row_ids]
        table_x = cell_table(weights[:, 0], local_x, span_cells)
        slope_x = cell_table(slopes[:, 0], local_x, span_cells)
        value_re = jnp.dot(table_x, near_re, precision=highest).reshape(-1, MY, KZW)
        value_im = jnp.dot(table_x, near_im, precision=highest).reshape(-1, MY, KZW)
        tilt_re = jnp.dot(slope_x, near_re, precision=highest).reshape(-1, MY, KZW)
        tilt_im = jnp.dot(slope_x, near_im, precision=highest).reshape(-1, MY, KZW)
        wave_y = wave_sums(weights[:, 1], base_now[1], modes_y, MY, 1.0)
        slope_y = wave_sums(slopes[:, 1], base_now[1], modes_y, MY, 1.0)
        wave_z = wave_sums(weights[:, 2], base_now[2], planes, MZ, 1.0)
        slope_z = wave_sums(slopes[:, 2], base_now[2], planes, MZ, 1.0)
        grad_x = projected(tilt_re, tilt_im, wave_y[0], wave_y[1], wave_z[0], wave_z[1])
        grad_y = projected(value_re, value_im, slope_y[0], slope_y[1], wave_z[0], wave_z[1])
        grad_z = projected(value_re, value_im, wave_y[0], wave_y[1], slope_z[0], slope_z[1])
        return -(charges_now / cell_size) * jnp.stack([grad_x, grad_y, grad_z])
    return lax.map(backward, jnp.arange(columns, dtype=jnp.int32))

def reference(node_state, mesh_base, mesh_frac, charge, nbr_code, nbr_count, radial_weight, mix_weight, force_weight):
    places = mesh_base.astype(jnp.float32) + mesh_frac
    updated, short_push = short_range(node_state, places, nbr_code, nbr_count, radial_weight, mix_weight, force_weight)
    long_push = long_range(mesh_base, mesh_frac, charge)
    node_next = updated.reshape(node_state.shape)
    forces = jnp.transpose(short_push + long_push, (1, 0, 2)).reshape(3, 2 * N_DX, 2 * N_DY, 2 * N_DZ, OCT)
    return (node_next, forces)
```

```python
import functools
import math

import jax
import jax.numpy as jnp
from jax import lax
from jax.experimental import pallas as pl
from jax.experimental.pallas import tpu as pltpu
from jax.sharding import PartitionSpec as P

NB = 8
NBR = 128
MB = 32
KZW = 8


cell_size = 1.13
ewald_beta = 0.625
coulomb = 332.0637
sigma_low = 8.0
sigma_rate = 1.5
highest = lax.Precision.HIGHEST


def spline_terms(fraction):
    remainder = 1.0 - fraction
    frac_square = fraction * fraction
    frac_cube = frac_square * fraction
    weights = jnp.stack(
        [
            remainder * remainder * remainder / 6.0,
            (3.0 * frac_cube - 6.0 * frac_square + 4.0) / 6.0,
            (-3.0 * frac_cube + 3.0 * frac_square + 3.0 * fraction + 1.0) / 6.0,
            frac_cube / 6.0,
        ]
    )
    slopes = jnp.stack(
        [
            -0.5 * remainder * remainder,
            1.5 * frac_square - 2.0 * fraction,
            -1.5 * frac_square + fraction + 0.5,
            0.5 * frac_square,
        ]
    )
    return (weights, slopes)


def spread_halo(block, width):
    for axis, dim in (("dx", 0), ("dy", 1), ("dz", 2)):
        count = lax.axis_size(axis)
        head = lax.slice_in_dim(block, 0, width, axis=dim)
        tail = lax.slice_in_dim(block, block.shape[dim] - width, block.shape[dim], axis=dim)
        block = jnp.concatenate(
            [
                lax.ppermute(tail, axis, [(i, (i + 1) % count) for i in range(count)]),
                block,
                lax.ppermute(head, axis, [((i + 1) % count, i) for i in range(count)]),
            ],
            axis=dim,
        )
    return block


def exact_pieces(values):
    pieces = []
    for _ in range(3):
        piece = lax.reduce_precision(values, 8, 7)
        pieces.append(piece.astype(jnp.bfloat16))
        values = values - piece
    return pieces


def pack_atoms(node_state, places):
    slots = node_state.shape[3]
    channels = node_state.shape[4]
    cells = jnp.concatenate(exact_pieces(places), axis=4)
    cells = jnp.transpose(cells, (1, 2, 3, 0, 4))
    cells = jnp.pad(cells, ((0, 0),) * 3 + ((0, 13), (0, channels - 3 * slots)))
    return jnp.concatenate([node_state, cells], axis=3)


def neighbour_kernel(
    sizes,
    packed_ref,
    code_ref,
    own_ref,
    radial_ref,
    mix_ref,
    force_ref,
    next_ref,
    push_ref,
    place_ref,
    state_ref,
    table_ref,
    count_ref,
    hot_ref,
    message_ref,
    *edge_refs,
):
    count_x, count_y, count_z, slots, basis = sizes
    octant = pl.program_id(0)
    columns = state_ref.shape[0]
    tiles = columns // 128
    per_tile = 128 // slots
    corner = ((octant // 4) * 4 + octant // 2 % 2) * 4 + octant % 2
    sides = [(side // 9 * 4 + side // 3 % 3) * 4 + side % 3 for side in range(27)]
    row_of = lax.broadcasted_iota(jnp.int32, (8, 128), 0)
    lane_of = lax.broadcasted_iota(jnp.int32, (8, 128), 1)

    @pl.when(octant == 0)
    def _():
        half = MB // 2
        state_ref[27 * slots :, :] = jnp.zeros((slots, 128), jnp.bfloat16)
        starts = [2 * lax.axis_index(axis) - 1 for axis in ("dx", "dy", "dz")]

        def unwrapped(place, start, count):
            reach = start + place
            below = jnp.where(reach < 0, -2 * count * half, 0)
            return jnp.where(reach >= 2 * count, 2 * count * half, below).astype(jnp.float32)

        @pl.loop(0, 64)
        def _(cell):
            rows = packed_ref[cell, slots : slots + 16, :].astype(jnp.float32)[:8]
            total = (rows + pltpu.roll(rows, 128 - slots, 1)) + pltpu.roll(rows, 128 - 2 * slots, 1)
            shift_x = unwrapped(cell // 16, starts[0], count_x)
            shift_y = unwrapped(cell // 4 % 4, starts[1], count_y)
            shift_z = unwrapped(cell % 4, starts[2], count_z)
            shift = jnp.where(row_of == 0, shift_x, jnp.where(row_of == 1, shift_y, shift_z))
            place_ref[cell] = total + shift

    for side in range(27):
        state_ref[side * slots : (side + 1) * slots, :] = packed_ref[corner + sides[side], :slots, :]
    for tile in range(tiles):
        joined = jnp.zeros((8, 128), jnp.float32)
        for part in range(per_tile):
            side = tile * per_tile + part
            if side < 27:
                moved = place_ref[corner + sides[side]]
                if part:
                    moved = pltpu.roll(moved, part * slots, 1)
                joined = jnp.where(lane_of // slots == part, moved, joined)
        table_ref[tile] = joined

    cell_iota = lax.broadcasted_iota(jnp.int32, (128, 128), 0).astype(jnp.float32).astype(jnp.bfloat16)
    one = jnp.ones((128, 128), jnp.bfloat16)
    zero = jnp.zeros((128, 128), jnp.bfloat16)
    for block in range(slots // 8):
        rows = slice(8 * block, 8 * block + 8)
        codes = code_ref[rows, :]
        live = lane_of.astype(jnp.float32) < own_ref[rows, 3:4]
        high = jnp.where(live, codes // 128, 64)
        low = (codes % 128).astype(jnp.float32)
        for atom in range(8):
            low_row = jnp.broadcast_to(low[atom : atom + 1], (16, 128)).astype(jnp.bfloat16)
            low_hot = jnp.where(cell_iota == jnp.concatenate([low_row] * 8, axis=0), one, zero)
            high_hot = (row_of == high[atom : atom + 1]).astype(jnp.float32).astype(jnp.bfloat16)
            count_ref[:, 8 * block + atom, :] = lax.dot_general(
                high_hot, low_hot, (((1,), (1,)), ((), ())), preferred_element_type=jnp.float32
            )
    lane_float = lane_of.astype(jnp.float32)
    for block in range(slots // 8):
        rows = slice(8 * block, 8 * block + 8)
        best = jnp.full((8, 128), -1.0, jnp.float32)
        for tile in range(tiles):
            times = count_ref[tile, rows, :]
            split = (times == 3.0) | ((times > 4.0) & (times < 8.0))
            best = jnp.where(split, lane_float + 128.0 * tile, best)
        chosen = jnp.max(best, axis=1, keepdims=True)
        rest = jnp.zeros((8, 128), jnp.float32)
        for tile in range(tiles):
            times = count_ref[tile, rows, :]
            hot = lane_float + 128.0 * tile == chosen
            part = jnp.where(times > 4.0, times - 4.0, times - 2.0)
            rest = rest + jnp.where(hot, part, 0.0)
            count_ref[tile, rows, :] = jnp.where(hot, times - part, times)
            hot_ref[rows, tile * 128 : tile * 128 + 128] = jnp.where(hot, 1.0, 0.0)
        total = jnp.sum(rest, axis=1, keepdims=True)
        spare = lane_of - (128 - slots) == row_of + 8 * block
        last = count_ref[tiles - 1, rows, :]
        count_ref[tiles - 1, rows, :] = jnp.where(spare, total, last)
    hots = hot_ref[...]
    state_ref[27 * slots :, :] = jnp.dot(
        hots.astype(jnp.bfloat16), state_ref[...], preferred_element_type=jnp.float32
    ).astype(jnp.bfloat16)
    spots = jnp.concatenate([table_ref[tile] for tile in range(tiles)], axis=1)
    found = lax.dot_general(
        spots, hots, (((1,), (1,)), ((), ())), precision=highest, preferred_element_type=jnp.float32
    )
    table_ref[tiles - 1] = jnp.where(
        lane_of < 128 - slots, table_ref[tiles - 1], jnp.concatenate([found] * per_tile, axis=1)
    )

    root_three = math.sqrt(3.0)
    root_fifteen = math.sqrt(15.0)
    root_five = math.sqrt(5.0)
    rates = [
        -(cell_size**2) / (sigma_low * sigma_rate**b) ** 2 * math.log2(math.e) for b in range(basis)
    ]
    for block in range(slots // 8):
        rows = slice(8 * block, 8 * block + 8)
        edge_ref = edge_refs[block % len(edge_refs)]
        own = own_ref[rows, :]
        for tile in range(tiles):
            times = count_ref[tile, rows, :]
            spots = table_ref[tile]
            dx = spots[0:1] - own[:, 0:1]
            dy = spots[1:2] - own[:, 1:2]
            dz = spots[2:3] - own[:, 2:3]
            square = dx * dx + dy * dy + dz * dz
            scale = lax.rsqrt(square + 1.0)
            ux = dx * scale
            uy = dy * scale
            uz = dz * scale
            tx = root_fifteen * ux
            angular = [
                None,
                root_three * ux,
                root_three * uy,
                root_three * uz,
                tx * uy,
                root_fifteen * uy * uz,
                0.5 * root_five * (3.0 * uz * uz - 1.0),
                tx * uz,
                0.5 * root_fifteen * (ux * ux - uy * uy),
            ]
            for pair in range(basis // 2):
                first = times * jnp.exp2(square * rates[2 * pair])
                second = times * jnp.exp2(square * rates[2 * pair + 1])
                for degree in range(9):
                    if degree:
                        parts = [first * angular[degree], second * angular[degree]]
                    else:
                        parts = [first, second]
                    at = (degree * basis + 2 * pair) * 8
                    edge_ref[at : at + 16, tile * 128 : tile * 128 + 128] = jnp.concatenate(
                        parts, axis=0
                    ).astype(jnp.bfloat16)
        summed = jnp.dot(edge_ref[...], state_ref[...], preferred_element_type=jnp.float32)
        for degree in range(9):
            total = summed[degree * basis * 8 : degree * basis * 8 + 8] * radial_ref[0:1, :]
            for b in range(1, basis):
                at = (degree * basis + b) * 8
                total = total + summed[at : at + 8] * radial_ref[b : b + 1, :]
            message_ref[degree, rows, :] = total / math.sqrt(NBR)
    message = message_ref[...].astype(jnp.bfloat16).reshape(9 * slots, 128)
    scalar = jnp.dot(message[:slots], mix_ref[0], preferred_element_type=jnp.float32)
    vector = jnp.dot(message[slots : 4 * slots], mix_ref[1], preferred_element_type=jnp.float32)
    tensor = jnp.dot(message[4 * slots :], mix_ref[2], preferred_element_type=jnp.float32)
    invariant = scalar
    squares = tensor * tensor
    for m in range(5):
        invariant = invariant + squares[m * slots : (m + 1) * slots]
    gating = 1.0 / (1.0 + jnp.exp(-invariant))
    own_state = packed_ref[corner + 21, :slots, :].astype(jnp.float32)
    next_ref[...] = (own_state + invariant * gating).astype(jnp.bfloat16)
    weighted = gating * force_ref[...]
    pushes = vector * jnp.concatenate([weighted] * 3, axis=0)
    push_ref[0] = lax.dot_general(
        jnp.ones((8, 128), jnp.float32),
        pushes,
        (((1,), (1,)), ((), ())),
        precision=highest,
        preferred_element_type=jnp.float32,
    )


def neighbour_sums(packed, nbr_code, own_rows, radial_weight, mix_weight, force_weight):
    slots = nbr_code.shape[3]
    channels = packed.shape[-1]
    basis = radial_weight.shape[0]
    columns = 28 * slots
    sizes = (lax.axis_size("dx"), lax.axis_size("dy"), lax.axis_size("dz"), slots, basis)
    edges = pltpu.VMEM((9 * basis * 8, columns), jnp.bfloat16)
    whole = lambda *shape: pl.BlockSpec(shape, lambda o: (0,) * len(shape))
    return pl.pallas_call(
        functools.partial(neighbour_kernel, sizes),
        grid=(8,),
        in_specs=[
            whole(64, slots + 16, channels),
            pl.BlockSpec((slots, NBR), lambda o: (o, 0)),
            pl.BlockSpec((slots, 4), lambda o: (o, 0)),
            whole(basis, channels),
            whole(3, channels, channels),
            whole(1, channels),
        ],
        out_specs=[
            pl.BlockSpec((slots, channels), lambda o: (o, 0)),
            pl.BlockSpec((1, 8, 3 * slots), lambda o: (o, 0, 0)),
        ],
        out_shape=[
            jax.ShapeDtypeStruct((8 * slots, channels), jnp.bfloat16),
            jax.ShapeDtypeStruct((8, 8, 3 * slots), jnp.float32),
        ],
        scratch_shapes=[
            pltpu.VMEM((64, 8, 128), jnp.float32),
            pltpu.VMEM((columns, channels), jnp.bfloat16),
            pltpu.VMEM((columns // 128, 8, 128), jnp.float32),
            pltpu.VMEM((8, slots, 128), jnp.float32),
            pltpu.VMEM((slots, columns), jnp.float32),
            pltpu.VMEM((9, slots, channels), jnp.float32),
            edges,
            edges,
        ],
        cost_estimate=pl.CostEstimate(flops=4_200_000_000, bytes_accessed=2_000_000, transcendentals=2_000_000),
    )(
        packed.reshape(64, slots + 16, channels),
        nbr_code.reshape(8 * slots, NBR),
        own_rows,
        radial_weight,
        mix_weight,
        force_weight[None],
    )


def phases(wavenumber, cell_index, extent):
    return 2.0 * math.pi / extent * jnp.mod(wavenumber * cell_index, extent).astype(jnp.float32)


def wave_sums(coeff, start_cells, wavenumber, extent, orient):
    wave_re = jnp.zeros((start_cells.shape[0], wavenumber.shape[0]), jnp.float32)
    wave_im = jnp.zeros((start_cells.shape[0], wavenumber.shape[0]), jnp.float32)
    for stencil in range(4):
        angles = phases(wavenumber[None, :], (start_cells + stencil)[:, None], extent)
        wave_re = wave_re + coeff[stencil][:, None] * jnp.cos(angles)
        wave_im = wave_im + coeff[stencil][:, None] * jnp.sin(angles)
    return (wave_re, orient * wave_im)


def cell_table(coeff, local_cells, cell_index):
    table = jnp.zeros((local_cells.shape[0], cell_index.shape[0]), jnp.float32)
    for stencil in range(4):
        match = (cell_index[None, :] == (local_cells + stencil)[:, None]).astype(jnp.float32)
        table = table + coeff[stencil][:, None] * match
    return table


def influence(modes_x, modes_y, modes_z, length_x, length_y, length_z):

    def folded(wavenumber, extent):
        return jnp.where(2 * wavenumber >= extent, wavenumber - extent, wavenumber).astype(
            jnp.float32
        ) / (cell_size * extent)

    wave_square = (
        jnp.square(folded(modes_x, length_x))
        + jnp.square(folded(modes_y, length_y))
        + jnp.square(folded(modes_z, length_z))
    )
    volume = cell_size**3 * length_x * length_y * length_z
    return (
        coulomb
        / (math.pi * volume)
        * jnp.exp(-math.pi**2 * wave_square / ewald_beta**2)
        / wave_square
    )


def projected(value_re, value_im, wave_y_re, wave_y_im, wave_z_re, wave_z_im):
    inner_re = jnp.sum(value_re * wave_y_re[:, :, None] - value_im * wave_y_im[:, :, None], axis=1)
    inner_im = jnp.sum(value_re * wave_y_im[:, :, None] + value_im * wave_y_re[:, :, None], axis=1)
    return 2.0 * jnp.sum(inner_re * wave_z_re - inner_im * wave_z_im, axis=1)


def shards(
    node_state,
    mesh_base,
    mesh_frac,
    charge,
    nbr_code,
    nbr_count,
    radial_weight,
    mix_weight,
    force_weight,
):
    count_x = lax.axis_size("dx")
    count_y = lax.axis_size("dy")
    count_z = lax.axis_size("dz")
    index_x = lax.axis_index("dx")
    index_y = lax.axis_index("dy")
    index_z = lax.axis_index("dz")
    octants = node_state.shape[3]
    channels = node_state.shape[4]
    atom_total = 8 * octants
    half_block = MB // 2
    block_cells = MB + 3
    length_x = MB * count_x
    length_y = MB * count_y
    length_z = MB * count_z
    places = mesh_base.astype(jnp.float32) + mesh_frac
    packed_halo = spread_halo(pack_atoms(node_state, places), 1)
    own_rows = jnp.transpose(
        jnp.concatenate([places, nbr_count.astype(jnp.float32)[None]], axis=0).reshape(4, atom_total)
    )
    updated, pushes = neighbour_sums(
        packed_halo, nbr_code, own_rows, radial_weight, mix_weight, force_weight
    )
    node_next = updated.reshape(node_state.shape)
    short_force = jnp.transpose(pushes[:, 0].reshape(8, 3, octants), (1, 0, 2)).reshape(3, atom_total)
    base_rows = mesh_base.reshape(3, atom_total)
    frac_rows = mesh_frac.reshape(3, atom_total)
    charge_rows = charge.reshape(atom_total)
    anchor_x = index_x * MB
    cell_index = jnp.arange(block_cells, dtype=jnp.int32)
    planes = 1 + jnp.arange(KZW, dtype=jnp.int32)
    rows_dev = MB * KZW // count_z
    row_start = (index_y * count_z + index_z) * rows_dev
    own_modes = row_start // KZW + jnp.arange(rows_dev // KZW, dtype=jnp.int32)
    modes_x = jnp.arange(length_x, dtype=jnp.int32)
    packed = jnp.concatenate([charge_rows[None], base_rows.astype(jnp.float32), frac_rows], axis=0)[
        None
    ]
    gathered = lax.all_gather(packed, ("dy", "dz"), axis=0, tiled=True)
    group_count = gathered.shape[0]
    group_size = math.gcd(group_count, 4)

    def bundle_modes(bundle):
        flat_rows = jnp.transpose(bundle, (1, 0, 2)).reshape(7, -1)
        charges_now = flat_rows[0]
        base_now = flat_rows[1:4].astype(jnp.int32)
        weights_now, slopes_now = spline_terms(flat_rows[4:7])
        table_now = cell_table(weights_now[:, 0], base_now[0] - anchor_x, cell_index)
        wave_y_re, wave_y_im = wave_sums(weights_now[:, 1], base_now[1], own_modes, length_y, -1.0)
        wave_z_re, wave_z_im = wave_sums(weights_now[:, 2], base_now[2], planes, length_z, -1.0)
        mixed_re = (
            wave_y_re[:, :, None] * wave_z_re[:, None, :]
            - wave_y_im[:, :, None] * wave_z_im[:, None, :]
        ).reshape(-1, rows_dev)
        mixed_im = (
            wave_y_re[:, :, None] * wave_z_im[:, None, :]
            + wave_y_im[:, :, None] * wave_z_re[:, None, :]
        ).reshape(-1, rows_dev)
        left_side = jnp.transpose(table_now * charges_now[:, None])
        return jnp.stack(
            [
                jnp.dot(left_side, mixed_re, precision=highest),
                jnp.dot(left_side, mixed_im, precision=highest),
            ],
            axis=1,
        )

    modes_sum = jnp.sum(
        lax.map(
            bundle_modes, gathered.reshape(group_count // group_size, group_size, 7, atom_total)
        ),
        axis=0,
    )
    slab_rows = jnp.transpose(modes_sum, (2, 1, 0))
    received = lax.all_gather(slab_rows[None], "dx", axis=0, tiled=True)
    shard_count = received.shape[0]
    cells_now = (jnp.arange(shard_count, dtype=jnp.int32) * MB)[:, None] + cell_index[None, :]
    angle_x = phases(cells_now.reshape(-1)[:, None], modes_x[None, :], length_x)
    cos_x = jnp.cos(angle_x)
    sin_x = jnp.sin(angle_x)
    lined_up = jnp.transpose(received, (1, 2, 0, 3)).reshape(received.shape[1], 2, -1)
    spec_re = jnp.dot(lined_up[:, 0], cos_x, precision=highest) + jnp.dot(
        lined_up[:, 1], sin_x, precision=highest
    )
    spec_im = jnp.dot(lined_up[:, 1], cos_x, precision=highest) - jnp.dot(
        lined_up[:, 0], sin_x, precision=highest
    )
    spectrum = jnp.stack([spec_re, spec_im], axis=1)
    global_rows = row_start + jnp.arange(rows_dev, dtype=jnp.int32)
    green_table = influence(
        modes_x[None, :],
        (global_rows // KZW)[:, None],
        (global_rows % KZW + 1)[:, None],
        length_x,
        length_y,
        length_z,
    )
    scaled = spectrum * green_table[:, None, :]
    angle_back = phases(modes_x[:, None], (anchor_x + cell_index)[None, :], length_x)
    cos_back = jnp.cos(angle_back)
    sin_back = jnp.sin(angle_back)
    back_re = jnp.dot(scaled[:, 0], cos_back, precision=highest) - jnp.dot(
        scaled[:, 1], sin_back, precision=highest
    )
    back_im = jnp.dot(scaled[:, 0], sin_back, precision=highest) + jnp.dot(
        scaled[:, 1], cos_back, precision=highest
    )
    back_re_cols = jnp.transpose(back_re)
    back_im_cols = jnp.transpose(back_im)
    wave_count = rows_dev // KZW
    bundle_size = math.gcd(lax.axis_size(("dy", "dz")) * 1, 4)

    def bundle_push(bundle):
        flat_rows = jnp.transpose(bundle, (1, 0, 2)).reshape(7, -1)
        charges_now = flat_rows[0]
        base_now = flat_rows[1:4].astype(jnp.int32)
        weights_now, slopes_now = spline_terms(flat_rows[4:7])
        table_now = cell_table(weights_now[:, 0], base_now[0] - anchor_x, cell_index)
        tilt_now = cell_table(slopes_now[:, 0], base_now[0] - anchor_x, cell_index)
        value_re = jnp.dot(table_now, back_re_cols, precision=highest).reshape(-1, wave_count, KZW)
        value_im = jnp.dot(table_now, back_im_cols, precision=highest).reshape(-1, wave_count, KZW)
        tilt_re = jnp.dot(tilt_now, back_re_cols, precision=highest).reshape(-1, wave_count, KZW)
        tilt_im = jnp.dot(tilt_now, back_im_cols, precision=highest).reshape(-1, wave_count, KZW)
        wave_y = wave_sums(weights_now[:, 1], base_now[1], own_modes, length_y, 1.0)
        slope_y = wave_sums(slopes_now[:, 1], base_now[1], own_modes, length_y, 1.0)
        wave_z = wave_sums(weights_now[:, 2], base_now[2], planes, length_z, 1.0)
        slope_z = wave_sums(slopes_now[:, 2], base_now[2], planes, length_z, 1.0)
        grad_x = projected(tilt_re, tilt_im, wave_y[0], wave_y[1], wave_z[0], wave_z[1])
        grad_y = projected(value_re, value_im, slope_y[0], slope_y[1], wave_z[0], wave_z[1])
        grad_z = projected(value_re, value_im, wave_y[0], wave_y[1], slope_z[0], slope_z[1])
        pushed = -(charges_now / cell_size) * jnp.stack([grad_x, grad_y, grad_z])
        return jnp.transpose(pushed.reshape(3, bundle_size, atom_total), (1, 0, 2))

    long_force = lax.psum_scatter(
        lax.map(
            bundle_push,
            gathered.reshape(
                lax.axis_size(("dy", "dz")) * 1 // bundle_size, bundle_size, 7, atom_total
            ),
        ).reshape(lax.axis_size(("dy", "dz")) * 1, 3, atom_total),
        ("dy", "dz"),
        scatter_dimension=0,
        tiled=True,
    )[0]
    forces = (short_force + long_force).reshape(3, 2, 2, 2, octants)
    return (node_next, forces)


def solution(mesh):
    placed = (
        P("dx", "dy", "dz", None, None),
        P(None, "dx", "dy", "dz", None),
        P(None, "dx", "dy", "dz", None),
        P("dx", "dy", "dz", None),
        P("dx", "dy", "dz", None, None),
        P("dx", "dy", "dz", None),
        P(),
        P(),
        P(),
    )
    return jax.shard_map(
        shards,
        mesh=mesh,
        in_specs=placed,
        out_specs=(P("dx", "dy", "dz", None, None), P(None, "dx", "dy", "dz", None)),
        check_vma=False,
    )
```

```python
import functools
import math

import jax
import jax.numpy as jnp
import numpy as np
from jax import lax
from jax.experimental import pallas as pl
from jax.experimental.pallas import tpu as pltpu
from jax.sharding import PartitionSpec as P

NB = 8
NBR = 128
MB = 32
KZW = 8


cell_size = 1.13
ewald_beta = 0.625
coulomb = 332.0637
sigma_low = 8.0
sigma_rate = 1.5
highest = lax.Precision.HIGHEST


def spread_halo(block, width):
    for axis, dim in (("dx", 0), ("dy", 1), ("dz", 2)):
        count = lax.axis_size(axis)
        head = lax.slice_in_dim(block, 0, width, axis=dim)
        tail = lax.slice_in_dim(block, block.shape[dim] - width, block.shape[dim], axis=dim)
        block = jnp.concatenate(
            [
                lax.ppermute(tail, axis, [(i, (i + 1) % count) for i in range(count)]),
                block,
                lax.ppermute(head, axis, [((i + 1) % count, i) for i in range(count)]),
            ],
            axis=dim,
        )
    return block


def exact_pieces(values):
    pieces = []
    for _ in range(3):
        piece = lax.reduce_precision(values, 8, 7)
        pieces.append(piece.astype(jnp.bfloat16))
        values = values - piece
    return pieces


def pack_atoms(node_state, places):
    slots = node_state.shape[3]
    channels = node_state.shape[4]
    cells = jnp.concatenate(exact_pieces(places), axis=4)
    cells = jnp.transpose(cells, (1, 2, 3, 0, 4))
    cells = jnp.pad(cells, ((0, 0),) * 3 + ((0, 13), (0, channels - 3 * slots)))
    return jnp.concatenate([node_state, cells], axis=3)


def neighbour_kernel(
    sizes,
    packed_ref,
    code_ref,
    own_ref,
    radial_ref,
    mix_ref,
    force_ref,
    next_ref,
    push_ref,
    place_ref,
    state_ref,
    table_ref,
    count_ref,
    hot_ref,
    message_ref,
    *edge_refs,
):
    count_x, count_y, count_z, slots, basis = sizes
    octant = pl.program_id(0)
    columns = state_ref.shape[0]
    tiles = columns // 128
    per_tile = 128 // slots
    corner = ((octant // 4) * 4 + octant // 2 % 2) * 4 + octant % 2
    sides = [(side // 9 * 4 + side // 3 % 3) * 4 + side % 3 for side in range(27)]
    row_of = lax.broadcasted_iota(jnp.int32, (8, 128), 0)
    lane_of = lax.broadcasted_iota(jnp.int32, (8, 128), 1)

    @pl.when(octant == 0)
    def _():
        half = MB // 2
        state_ref[27 * slots :, :] = jnp.zeros((slots, 128), jnp.bfloat16)
        starts = [2 * lax.axis_index(axis) - 1 for axis in ("dx", "dy", "dz")]

        def unwrapped(place, start, count):
            reach = start + place
            below = jnp.where(reach < 0, -2 * count * half, 0)
            return jnp.where(reach >= 2 * count, 2 * count * half, below).astype(jnp.float32)

        @pl.loop(0, 64)
        def _(cell):
            rows = packed_ref[cell, slots : slots + 16, :].astype(jnp.float32)[:8]
            total = (rows + pltpu.roll(rows, 128 - slots, 1)) + pltpu.roll(rows, 128 - 2 * slots, 1)
            shift_x = unwrapped(cell // 16, starts[0], count_x)
            shift_y = unwrapped(cell // 4 % 4, starts[1], count_y)
            shift_z = unwrapped(cell % 4, starts[2], count_z)
            shift = jnp.where(row_of == 0, shift_x, jnp.where(row_of == 1, shift_y, shift_z))
            place_ref[cell] = total + shift

    for side in range(27):
        state_ref[side * slots : (side + 1) * slots, :] = packed_ref[corner + sides[side], :slots, :]
    for tile in range(tiles):
        joined = jnp.zeros((8, 128), jnp.float32)
        for part in range(per_tile):
            side = tile * per_tile + part
            if side < 27:
                moved = place_ref[corner + sides[side]]
                if part:
                    moved = pltpu.roll(moved, part * slots, 1)
                joined = jnp.where(lane_of // slots == part, moved, joined)
        table_ref[tile] = joined

    cell_iota = lax.broadcasted_iota(jnp.int32, (128, 128), 0).astype(jnp.float32).astype(jnp.bfloat16)
    one = jnp.ones((128, 128), jnp.bfloat16)
    zero = jnp.zeros((128, 128), jnp.bfloat16)
    for block in range(slots // 8):
        rows = slice(8 * block, 8 * block + 8)
        codes = code_ref[rows, :]
        live = lane_of.astype(jnp.float32) < own_ref[rows, 3:4]
        high = jnp.where(live, codes // 128, 64)
        low = (codes % 128).astype(jnp.float32)
        for atom in range(8):
            low_row = jnp.broadcast_to(low[atom : atom + 1], (16, 128)).astype(jnp.bfloat16)
            low_hot = jnp.where(cell_iota == jnp.concatenate([low_row] * 8, axis=0), one, zero)
            high_hot = (row_of == high[atom : atom + 1]).astype(jnp.float32).astype(jnp.bfloat16)
            count_ref[:, 8 * block + atom, :] = lax.dot_general(
                high_hot, low_hot, (((1,), (1,)), ((), ())), preferred_element_type=jnp.float32
            )
    lane_float = lane_of.astype(jnp.float32)
    for block in range(slots // 8):
        rows = slice(8 * block, 8 * block + 8)
        best = jnp.full((8, 128), -1.0, jnp.float32)
        for tile in range(tiles):
            times = count_ref[tile, rows, :]
            split = (times == 3.0) | ((times > 4.0) & (times < 8.0))
            best = jnp.where(split, lane_float + 128.0 * tile, best)
        chosen = jnp.max(best, axis=1, keepdims=True)
        rest = jnp.zeros((8, 128), jnp.float32)
        for tile in range(tiles):
            times = count_ref[tile, rows, :]
            hot = lane_float + 128.0 * tile == chosen
            part = jnp.where(times > 4.0, times - 4.0, times - 2.0)
            rest = rest + jnp.where(hot, part, 0.0)
            count_ref[tile, rows, :] = jnp.where(hot, times - part, times)
            hot_ref[rows, tile * 128 : tile * 128 + 128] = jnp.where(hot, 1.0, 0.0)
        total = jnp.sum(rest, axis=1, keepdims=True)
        spare = lane_of - (128 - slots) == row_of + 8 * block
        last = count_ref[tiles - 1, rows, :]
        count_ref[tiles - 1, rows, :] = jnp.where(spare, total, last)
    hots = hot_ref[...]
    state_ref[27 * slots :, :] = jnp.dot(
        hots.astype(jnp.bfloat16), state_ref[...], preferred_element_type=jnp.float32
    ).astype(jnp.bfloat16)
    spots = jnp.concatenate([table_ref[tile] for tile in range(tiles)], axis=1)
    found = lax.dot_general(
        spots, hots, (((1,), (1,)), ((), ())), precision=highest, preferred_element_type=jnp.float32
    )
    table_ref[tiles - 1] = jnp.where(
        lane_of < 128 - slots, table_ref[tiles - 1], jnp.concatenate([found] * per_tile, axis=1)
    )

    root_three = math.sqrt(3.0)
    root_fifteen = math.sqrt(15.0)
    root_five = math.sqrt(5.0)
    rates = [
        -(cell_size**2) / (sigma_low * sigma_rate**b) ** 2 * math.log2(math.e) for b in range(basis)
    ]
    for block in range(slots // 8):
        rows = slice(8 * block, 8 * block + 8)
        edge_ref = edge_refs[block % len(edge_refs)]
        own = own_ref[rows, :]
        for tile in range(tiles):
            times = count_ref[tile, rows, :]
            spots = table_ref[tile]
            dx = spots[0:1] - own[:, 0:1]
            dy = spots[1:2] - own[:, 1:2]
            dz = spots[2:3] - own[:, 2:3]
            square = dx * dx + dy * dy + dz * dz
            scale = lax.rsqrt(square + 1.0)
            ux = dx * scale
            uy = dy * scale
            uz = dz * scale
            tx = root_fifteen * ux
            angular = [
                None,
                root_three * ux,
                root_three * uy,
                root_three * uz,
                tx * uy,
                root_fifteen * uy * uz,
                0.5 * root_five * (3.0 * uz * uz - 1.0),
                tx * uz,
                0.5 * root_fifteen * (ux * ux - uy * uy),
            ]
            for pair in range(basis // 2):
                first = times * jnp.exp2(square * rates[2 * pair])
                second = times * jnp.exp2(square * rates[2 * pair + 1])
                for degree in range(9):
                    if degree:
                        parts = [first * angular[degree], second * angular[degree]]
                    else:
                        parts = [first, second]
                    at = (degree * basis + 2 * pair) * 8
                    edge_ref[at : at + 16, tile * 128 : tile * 128 + 128] = jnp.concatenate(
                        parts, axis=0
                    ).astype(jnp.bfloat16)
        summed = jnp.dot(edge_ref[...], state_ref[...], preferred_element_type=jnp.float32)
        for degree in range(9):
            total = summed[degree * basis * 8 : degree * basis * 8 + 8] * radial_ref[0:1, :]
            for b in range(1, basis):
                at = (degree * basis + b) * 8
                total = total + summed[at : at + 8] * radial_ref[b : b + 1, :]
            message_ref[degree, rows, :] = total / math.sqrt(NBR)
    message = message_ref[...].astype(jnp.bfloat16).reshape(9 * slots, 128)
    scalar = jnp.dot(message[:slots], mix_ref[0], preferred_element_type=jnp.float32)
    vector = jnp.dot(message[slots : 4 * slots], mix_ref[1], preferred_element_type=jnp.float32)
    tensor = jnp.dot(message[4 * slots :], mix_ref[2], preferred_element_type=jnp.float32)
    invariant = scalar
    squares = tensor * tensor
    for m in range(5):
        invariant = invariant + squares[m * slots : (m + 1) * slots]
    gating = 1.0 / (1.0 + jnp.exp(-invariant))
    own_state = packed_ref[corner + 21, :slots, :].astype(jnp.float32)
    next_ref[...] = (own_state + invariant * gating).astype(jnp.bfloat16)
    weighted = gating * force_ref[...]
    pushes = vector * jnp.concatenate([weighted] * 3, axis=0)
    push_ref[0] = lax.dot_general(
        jnp.ones((8, 128), jnp.float32),
        pushes,
        (((1,), (1,)), ((), ())),
        precision=highest,
        preferred_element_type=jnp.float32,
    )


def neighbour_sums(packed, nbr_code, own_rows, radial_weight, mix_weight, force_weight):
    slots = nbr_code.shape[3]
    channels = packed.shape[-1]
    basis = radial_weight.shape[0]
    columns = 28 * slots
    sizes = (lax.axis_size("dx"), lax.axis_size("dy"), lax.axis_size("dz"), slots, basis)
    edges = pltpu.VMEM((9 * basis * 8, columns), jnp.bfloat16)
    whole = lambda *shape: pl.BlockSpec(shape, lambda o: (0,) * len(shape))
    return pl.pallas_call(
        functools.partial(neighbour_kernel, sizes),
        grid=(8,),
        in_specs=[
            whole(64, slots + 16, channels),
            pl.BlockSpec((slots, NBR), lambda o: (o, 0)),
            pl.BlockSpec((slots, 4), lambda o: (o, 0)),
            whole(basis, channels),
            whole(3, channels, channels),
            whole(1, channels),
        ],
        out_specs=[
            pl.BlockSpec((slots, channels), lambda o: (o, 0)),
            pl.BlockSpec((1, 8, 3 * slots), lambda o: (o, 0, 0)),
        ],
        out_shape=[
            jax.ShapeDtypeStruct((8 * slots, channels), jnp.bfloat16),
            jax.ShapeDtypeStruct((8, 8, 3 * slots), jnp.float32),
        ],
        scratch_shapes=[
            pltpu.VMEM((64, 8, 128), jnp.float32),
            pltpu.VMEM((columns, channels), jnp.bfloat16),
            pltpu.VMEM((columns // 128, 8, 128), jnp.float32),
            pltpu.VMEM((8, slots, 128), jnp.float32),
            pltpu.VMEM((slots, columns), jnp.float32),
            pltpu.VMEM((9, slots, channels), jnp.float32),
            edges,
            edges,
        ],
        cost_estimate=pl.CostEstimate(flops=4_200_000_000, bytes_accessed=2_000_000, transcendentals=2_000_000),
    )(
        packed.reshape(64, slots + 16, channels),
        nbr_code.reshape(8 * slots, NBR),
        own_rows,
        radial_weight,
        mix_weight,
        force_weight[None],
    )


def spline_rows(fraction):
    remainder = 1.0 - fraction
    square = fraction * fraction
    cube = square * fraction
    weights = [
        remainder * remainder * remainder / 6.0,
        (3.0 * cube - 6.0 * square + 4.0) / 6.0,
        (-3.0 * cube + 3.0 * square + 3.0 * fraction + 1.0) / 6.0,
        cube / 6.0,
    ]
    slopes = [
        -0.5 * remainder * remainder,
        1.5 * square - 2.0 * fraction,
        -1.5 * square + fraction + 0.5,
        0.5 * square,
    ]
    return weights, slopes


def turn(table_ref, steps, extent):
    def look(index):
        index = index % extent
        rows, width = index.shape
        found = []
        for start in range(0, width, 128):
            piece = index[:, start : start + 128]
            result = None
            for part in range(-(-extent // 128)):
                line = jnp.broadcast_to(table_ref[part : part + 1, :], piece.shape)
                here = jnp.take_along_axis(line, piece % 128, axis=1)
                result = here if result is None else jnp.where(piece // 128 == part, here, result)
            found.append(result)
        return jnp.concatenate(found, axis=1) if len(found) > 1 else found[0]

    return look(steps), look(steps + 3 * extent // 4)


def wave_factors(table_ref, modes, base_row, extent):
    rows = modes.shape[0]
    width = base_row.shape[1]
    wide = jnp.broadcast_to(modes[:, :1], (rows, width))
    first = turn(table_ref, wide * base_row, extent)
    steps = [turn(table_ref, modes * t, extent) for t in (1, 2, 3)]
    steps = [tuple(jnp.concatenate([p] * (width // 128), axis=1) for p in pair) for pair in steps]
    return first, steps


def wave_of(factors, coeff):
    (cos_first, sin_first), steps = factors
    part_re = coeff[0] + coeff[1] * steps[0][0] + coeff[2] * steps[1][0] + coeff[3] * steps[2][0]
    part_im = coeff[1] * steps[0][1] + coeff[2] * steps[1][1] + coeff[3] * steps[2][1]
    return cos_first * part_re - sin_first * part_im, sin_first * part_re + cos_first * part_im


def cell_rows(coeff, local_row, cells):
    row_of = lax.broadcasted_iota(jnp.int32, (cells, local_row.shape[1]), 0)
    away = row_of - local_row
    table = jnp.where(away == 3, coeff[3], 0.0)
    for stencil in (2, 1, 0):
        table = jnp.where(away == stencil, coeff[stencil], table)
    return table


def halves(values):
    high = values.astype(jnp.bfloat16).astype(jnp.float32)
    return high, values - high


def wave_start():
    return lax.axis_index("dy") * lax.axis_size("dz") + lax.axis_index("dz")


def spread_kernel(sizes, atoms_ref, table_y_ref, table_z_ref, sums_ref):
    length_y, length_z, waves, cells = sizes
    groups, _, width = atoms_ref.shape
    modes_y = wave_start() * waves + lax.broadcasted_iota(jnp.int32, (waves, 128), 0)
    modes_z = 1 + lax.broadcasted_iota(jnp.int32, (KZW, 128), 0)
    anchor = lax.axis_index("dx") * MB
    total = jnp.zeros(sums_ref.shape, jnp.float32)
    for group in range(groups):
        chunk = atoms_ref[group]
        base = chunk[1:4].astype(jnp.int32)
        weights, _ = spline_rows(chunk[4:7])
        row = lambda d: [w[d : d + 1] for w in weights]
        y_re, y_im = wave_of(wave_factors(table_y_ref, modes_y, base[1:2], length_y), row(1))
        z_re, z_im = wave_of(wave_factors(table_z_ref, modes_z, base[2:3], length_z), row(2))
        mixed_re = []
        mixed_im = []
        for k in range(waves):
            k_re = y_re[k : k + 1]
            k_im = y_im[k : k + 1]
            mixed_re.append(k_re * z_re - k_im * z_im)
            mixed_im.append(-(k_re * z_im + k_im * z_re))
        mixed = jnp.concatenate(mixed_re + mixed_im, axis=0)
        table = cell_rows(row(0), base[0:1] - anchor, cells) * chunk[0:1]
        table_high, table_low = halves(table)
        mixed_high, mixed_low = halves(mixed)
        both = jnp.concatenate([table_high, table_low], axis=0).astype(jnp.bfloat16)
        main = lax.dot_general(
            both,
            mixed_high.astype(jnp.bfloat16),
            (((1,), (1,)), ((), ())),
            preferred_element_type=jnp.float32,
        )
        side = lax.dot_general(
            table_high.astype(jnp.bfloat16),
            mixed_low.astype(jnp.bfloat16),
            (((1,), (1,)), ((), ())),
            preferred_element_type=jnp.float32,
        )
        total = total + (main[:cells] + (main[cells:] + side))
    sums_ref[...] = total


def push_kernel(
    sizes, atoms_ref, sums_ref, forward_ref, back_ref, table_y_ref, table_z_ref, force_ref
):
    length_x, length_y, length_z, waves, cells = sizes
    groups, _, width = atoms_ref.shape
    modes = waves * KZW
    start = wave_start() * waves
    modes_y = start + lax.broadcasted_iota(jnp.int32, (waves, 128), 0)
    modes_z = 1 + lax.broadcasted_iota(jnp.int32, (KZW, 128), 0)
    anchor = lax.axis_index("dx") * MB

    turned = jnp.dot(
        forward_ref[...], sums_ref[...], precision=highest, preferred_element_type=jnp.float32
    )
    cosine = turned[:length_x]
    sine = turned[length_x:]

    def folded(number, extent):
        number = jnp.where(2 * number >= extent, number - extent, number)
        return number.astype(jnp.float32) / (cell_size * extent)

    mode_shape = (length_x, modes)
    mode_x = lax.broadcasted_iota(jnp.int32, mode_shape, 0)
    mode_lane = lax.broadcasted_iota(jnp.int32, mode_shape, 1)
    wave_square = (
        jnp.square(folded(mode_x, length_x))
        + jnp.square(folded(start + mode_lane // KZW, length_y))
        + jnp.square(folded(mode_lane % KZW + 1, length_z))
    )
    volume = cell_size**3 * length_x * length_y * length_z
    green = (
        coulomb
        / (math.pi * volume)
        * jnp.exp(-(math.pi**2) * wave_square / ewald_beta**2)
        / wave_square
    )
    scaled = jnp.concatenate(
        [
            green * (cosine[:, :modes] + sine[:, modes:]),
            green * (cosine[:, modes:] - sine[:, :modes]),
        ],
        axis=1,
    )
    lines = back_ref[pl.ds(pl.multiple_of(lax.axis_index("dx") * cells, 8), cells), :]
    lines = jnp.concatenate([lines[:, :length_x], lines[:, length_x:]], axis=0)
    turned = jnp.dot(lines, scaled, precision=highest, preferred_element_type=jnp.float32)
    cosine = turned[:cells]
    sine = turned[cells:]
    back = jnp.concatenate(
        [cosine[:, :modes] - sine[:, modes:], sine[:, :modes] + cosine[:, modes:]], axis=1
    )
    back_high, back_low = halves(back)
    spare = jnp.zeros((128 - 3 * cells, 2 * modes), jnp.float32)
    stacked = jnp.concatenate([back_high, back_high, back_low, spare], axis=0)
    stacked = jnp.transpose(stacked).astype(jnp.bfloat16)

    for group in range(groups):
        chunk = atoms_ref[group]
        base = chunk[1:4].astype(jnp.int32)
        weights, slopes = spline_rows(chunk[4:7])
        row = lambda d: [w[d : d + 1] for w in weights]
        tilt = lambda d: [w[d : d + 1] for w in slopes]
        factors_y = wave_factors(table_y_ref, modes_y, base[1:2], length_y)
        factors_z = wave_factors(table_z_ref, modes_z, base[2:3], length_z)
        y_re, y_im = wave_of(factors_y, row(1))
        dy_re, dy_im = wave_of(factors_y, tilt(1))
        z_re, z_im = wave_of(factors_z, row(2))
        dz_re, dz_im = wave_of(factors_z, tilt(2))

        def on_atoms(coeff):
            high, low = halves(cell_rows(coeff, base[0:1] - anchor, cells))
            none = jnp.zeros((128 - 3 * cells, width), jnp.float32)
            right = jnp.concatenate([high, low, high, none], axis=0).astype(jnp.bfloat16)
            return jnp.dot(stacked, right, preferred_element_type=jnp.float32)

        value = on_atoms(row(0))
        slant = on_atoms(tilt(0))

        def along(field, wave_re, wave_im):
            sum_re = jnp.zeros((KZW, width), jnp.float32)
            sum_im = jnp.zeros((KZW, width), jnp.float32)
            for k in range(waves):
                f_re = field[k * KZW : (k + 1) * KZW]
                f_im = field[modes + k * KZW : modes + (k + 1) * KZW]
                k_re = wave_re[k : k + 1]
                k_im = wave_im[k : k + 1]
                sum_re = sum_re + (f_re * k_re - f_im * k_im)
                sum_im = sum_im + (f_re * k_im + f_im * k_re)
            return sum_re, sum_im

        def ended(pair, wave_re, wave_im):
            return 2.0 * jnp.sum(pair[0] * wave_re - pair[1] * wave_im, axis=0, keepdims=True)

        push_x = ended(along(slant, y_re, y_im), z_re, z_im)
        push_y = ended(along(value, dy_re, dy_im), z_re, z_im)
        push_z = ended(along(value, y_re, y_im), dz_re, dz_im)
        force_ref[group] = jnp.concatenate([push_x, push_y, push_z], axis=0) * (
            -chunk[0:1] / cell_size
        )


def cosine_period(extent):
    lines = -(-extent // 128)
    steps = np.arange(lines * 128).reshape(lines, 128)
    return jnp.asarray(np.cos(2.0 * np.pi * steps / extent).astype(np.float32))


def long_range(mesh_base, mesh_frac, charge):
    count_x = lax.axis_size("dx")
    count_y = lax.axis_size("dy")
    count_z = lax.axis_size("dz")
    atom_total = charge.size
    groups = count_y * count_z
    cells = -(-(MB + 3) // 8) * 8
    length_x = MB * count_x
    length_y = MB * count_y
    length_z = MB * count_z
    waves = MB // count_z
    modes = waves * KZW
    packed = jnp.concatenate(
        [
            charge.reshape(1, atom_total),
            mesh_base.reshape(3, atom_total).astype(jnp.float32),
            mesh_frac.reshape(3, atom_total),
        ],
        axis=0,
    )
    atoms = lax.all_to_all(
        jnp.broadcast_to(packed[None], (groups, 7, atom_total)), ("dy", "dz"), 0, 0, tiled=True
    )
    table_y = cosine_period(length_y)
    table_z = cosine_period(length_z)
    sums = pl.pallas_call(
        functools.partial(spread_kernel, (length_y, length_z, waves, cells)),
        out_shape=jax.ShapeDtypeStruct((cells, 2 * modes), jnp.float32),
    )(atoms, table_y, table_z)
    received = lax.all_to_all(
        jnp.broadcast_to(sums[None], (count_x,) + sums.shape), "dx", 0, 0, tiled=True
    ).reshape(count_x * cells, 2 * modes)
    places = (np.arange(count_x) * MB)[:, None] + np.arange(cells)[None, :]
    angles = 2.0 * np.pi / length_x * (np.arange(length_x)[:, None] * places.reshape(1, -1) % length_x)
    forward = np.concatenate([np.cos(angles), np.sin(angles)], axis=0).astype(np.float32)
    parts = pl.pallas_call(
        functools.partial(push_kernel, (length_x, length_y, length_z, waves, cells)),
        out_shape=jax.ShapeDtypeStruct((groups, 3, atom_total), jnp.float32),
    )(atoms, received, jnp.asarray(forward), jnp.asarray(forward.T.copy()), table_y, table_z)
    parts = lax.all_to_all(parts, ("dy", "dz"), 0, 0, tiled=True)
    return jnp.sum(parts, axis=0)


def shards(
    node_state,
    mesh_base,
    mesh_frac,
    charge,
    nbr_code,
    nbr_count,
    radial_weight,
    mix_weight,
    force_weight,
):
    octants = node_state.shape[3]
    atom_total = 8 * octants
    places = mesh_base.astype(jnp.float32) + mesh_frac
    packed_halo = spread_halo(pack_atoms(node_state, places), 1)
    own_rows = jnp.transpose(
        jnp.concatenate([places, nbr_count.astype(jnp.float32)[None]], axis=0).reshape(4, atom_total)
    )
    updated, pushes = neighbour_sums(
        packed_halo, nbr_code, own_rows, radial_weight, mix_weight, force_weight
    )
    node_next = updated.reshape(node_state.shape)
    short_force = jnp.transpose(pushes[:, 0].reshape(8, 3, octants), (1, 0, 2)).reshape(3, atom_total)
    long_force = long_range(mesh_base, mesh_frac, charge)
    forces = (short_force + long_force).reshape(3, 2, 2, 2, octants)
    return (node_next, forces)


def solution(mesh):
    placed = (
        P("dx", "dy", "dz", None, None),
        P(None, "dx", "dy", "dz", None),
        P(None, "dx", "dy", "dz", None),
        P("dx", "dy", "dz", None),
        P("dx", "dy", "dz", None, None),
        P("dx", "dy", "dz", None),
        P(),
        P(),
        P(),
    )
    return jax.shard_map(
        shards,
        mesh=mesh,
        in_specs=placed,
        out_specs=(P("dx", "dy", "dz", None, None), P(None, "dx", "dy", "dz", None)),
        check_vma=False,
    )
```

```python
import functools
import math

import jax
import jax.numpy as jnp
import numpy as np
from jax import lax
from jax.experimental import pallas as pl
from jax.experimental.pallas import tpu as pltpu
from jax.sharding import PartitionSpec as P


NBR = 128
MB = 32
KZW = 8


cell_size = 1.13
ewald_beta = 0.625
coulomb = 332.0637
sigma_low = 8.0
sigma_rate = 1.5
highest = lax.Precision.HIGHEST


def spread_halo(block, width):
    for axis, dim in (("dx", 0), ("dy", 1), ("dz", 2)):
        count = lax.axis_size(axis)
        head = lax.slice_in_dim(block, 0, width, axis=dim)
        tail = lax.slice_in_dim(block, block.shape[dim] - width, block.shape[dim], axis=dim)
        below = lax.ppermute(tail, axis, [(i, (i + 1) % count) for i in range(count)])
        above = lax.ppermute(head, axis, [((i + 1) % count, i) for i in range(count)])
        block = jnp.concatenate([below, block, above], axis=dim)
    return block


def exact_pieces(values):
    pieces = []
    for _ in range(3):
        piece = lax.reduce_precision(values, 8, 7)
        pieces.append(piece.astype(jnp.bfloat16))
        values = values - piece
    return pieces


def pack_atoms(node_state, places):
    slots = node_state.shape[3]
    channels = node_state.shape[4]
    cells = jnp.concatenate(exact_pieces(places), axis=4)
    cells = jnp.transpose(cells, (1, 2, 3, 0, 4))
    cells = jnp.pad(cells, ((0, 0),) * 3 + ((0, 13), (0, channels - 3 * slots)))
    return jnp.concatenate([node_state, cells], axis=3)


def count_kernel(code_ref, own_ref, count_ref, chosen_ref):
    slots = code_ref.shape[0]
    tiles = count_ref.shape[1]
    row_of = lax.broadcasted_iota(jnp.int32, (8, 128), 0)
    lane_of = lax.broadcasted_iota(jnp.int32, (8, 128), 1)
    cell_iota = lax.broadcasted_iota(jnp.int32, (128, 128), 0).astype(jnp.float32).astype(jnp.bfloat16)
    one = jnp.ones((128, 128), jnp.bfloat16)
    zero = jnp.zeros((128, 128), jnp.bfloat16)
    lane_float = lane_of.astype(jnp.float32)
    for block in range(slots // 8):
        rows = slice(8 * block, 8 * block + 8)
        codes = code_ref[rows, :]
        live = lane_float < own_ref[rows, 3:4]
        high = jnp.where(live, codes // 128, 64)
        low = (codes % 128).astype(jnp.float32)
        for atom in range(8):
            low_row = jnp.broadcast_to(low[atom : atom + 1], (16, 128)).astype(jnp.bfloat16)
            low_hot = jnp.where(cell_iota == jnp.concatenate([low_row] * 8, axis=0), one, zero)
            high_hot = (row_of == high[atom : atom + 1]).astype(jnp.float32).astype(jnp.bfloat16)
            counted = lax.dot_general(
                high_hot, low_hot, (((1,), (1,)), ((), ())), preferred_element_type=jnp.float32
            )
            count_ref[0, :, 8 * block + atom, :] = counted[:tiles]
    for block in range(slots // 8):
        rows = slice(8 * block, 8 * block + 8)
        best = jnp.full((8, 128), -1.0, jnp.float32)
        for tile in range(tiles):
            times = count_ref[0, tile, rows, :]
            split = (times == 3.0) | ((times > 4.0) & (times < 8.0))
            best = jnp.where(split, lane_float + 128.0 * tile, best)
        chosen = jnp.max(best, axis=1, keepdims=True)
        chosen_ref[rows, :] = jnp.broadcast_to(chosen, (8, 128))
        rest = jnp.zeros((8, 128), jnp.float32)
        for tile in range(tiles):
            times = count_ref[0, tile, rows, :]
            hot = lane_float + 128.0 * tile == chosen
            part = jnp.where(times > 4.0, times - 4.0, times - 2.0)
            rest = rest + jnp.where(hot, part, 0.0)
            count_ref[0, tile, rows, :] = jnp.where(hot, times - part, times)
        total = jnp.sum(rest, axis=1, keepdims=True)
        spare = lane_of - (128 - slots) == row_of + 8 * block
        last = count_ref[0, tiles - 1, rows, :]
        count_ref[0, tiles - 1, rows, :] = jnp.where(spare, total, last)


def neighbour_kernel(
    sizes,
    packed_ref,
    count_ref,
    chosen_ref,
    own_ref,
    radial_ref,
    mix_ref,
    force_ref,
    next_ref,
    push_ref,
    place_ref,
    state_ref,
    table_ref,
    message_ref,
    *edge_refs,
):
    count_x, count_y, count_z, slots, basis = sizes
    octant = pl.program_id(0)
    columns = state_ref.shape[1]
    tiles = columns // 128
    per_tile = 128 // slots
    blocks = slots // 8
    atoms = 8 * slots
    corner = ((octant // 4) * 4 + octant // 2 % 2) * 4 + octant % 2
    sides = [(side // 9 * 4 + side // 3 % 3) * 4 + side % 3 for side in range(27)]
    row_of = lax.broadcasted_iota(jnp.int32, (8, 128), 0)
    lane_of = lax.broadcasted_iota(jnp.int32, (8, 128), 1)
    lane_float = lane_of.astype(jnp.float32)
    here = octant % 2
    before = 1 - here

    @pl.when(octant == 0)
    def _():
        half = MB // 2
        for parity in range(2):
            state_ref[parity, 27 * slots :, :] = jnp.zeros((slots, 128), jnp.bfloat16)
        starts = [2 * lax.axis_index(axis) - 1 for axis in ("dx", "dy", "dz")]

        def unwrapped(place, start, count):
            reach = start + place
            below = jnp.where(reach < 0, -2 * count * half, 0)
            return jnp.where(reach >= 2 * count, 2 * count * half, below).astype(jnp.float32)

        @pl.loop(0, 64, unroll=8)
        def _(cell):
            rows = packed_ref[cell, slots : slots + 16, :].astype(jnp.float32)[:8]
            total = (rows + pltpu.roll(rows, 128 - slots, 1)) + pltpu.roll(rows, 128 - 2 * slots, 1)
            shift_x = unwrapped(cell // 16, starts[0], count_x)
            shift_y = unwrapped(cell // 4 % 4, starts[1], count_y)
            shift_z = unwrapped(cell % 4, starts[2], count_z)
            shift = jnp.where(row_of == 0, shift_x, jnp.where(row_of == 1, shift_y, shift_z))
            place_ref[cell] = total + shift

    for side in range(27):
        state_ref[here, side * slots : (side + 1) * slots, :] = packed_ref[
            corner + sides[side], :slots, :
        ]
    for tile in range(tiles):
        joined = jnp.zeros((8, 128), jnp.float32)
        for part in range(per_tile):
            side = tile * per_tile + part
            if side < 27:
                moved = place_ref[corner + sides[side]]
                if part:
                    moved = pltpu.roll(moved, part * slots, 1)
                joined = jnp.where(lane_of // slots == part, moved, joined)
        table_ref[tile] = joined

    chosen = chosen_ref[...]
    wide_lane = lax.broadcasted_iota(jnp.int32, (slots, 128), 1).astype(jnp.float32)
    hots = jnp.concatenate(
        [jnp.where(wide_lane + 128.0 * tile == chosen, 1.0, 0.0) for tile in range(tiles)], axis=1
    ).astype(jnp.bfloat16)
    state_ref[here, 27 * slots :, :] = jnp.dot(
        hots, state_ref[here], preferred_element_type=jnp.float32
    ).astype(jnp.bfloat16)
    pieces = []
    spots = jnp.concatenate([table_ref[tile] for tile in range(tiles)], axis=1)
    for _ in range(3):
        piece = spots.astype(jnp.bfloat16).astype(jnp.float32)
        pieces.append(piece)
        spots = spots - piece
    pieces = jnp.concatenate(pieces + [jnp.zeros_like(spots)], axis=0).astype(jnp.bfloat16)
    found = lax.dot_general(
        pieces, hots, (((1,), (1,)), ((), ())), preferred_element_type=jnp.float32
    )
    found = (found[:8] + found[8:16]) + found[16:24]
    table_ref[tiles - 1] = jnp.where(
        lane_of < 128 - slots, table_ref[tiles - 1], jnp.concatenate([found] * per_tile, axis=1)
    )

    root_three = math.sqrt(3.0)
    root_fifteen = math.sqrt(15.0)
    root_five = math.sqrt(5.0)
    rates = [
        -(cell_size**2) / (sigma_low * sigma_rate**b) ** 2 * math.log2(math.e) for b in range(basis)
    ]

    def fill_edges(block):
        rows = slice(8 * block, 8 * block + 8)
        edge_ref = edge_refs[block % 2]
        own = own_ref[rows, :]
        for tile in range(tiles):
            times = count_ref[0, tile, rows, :]
            spots = table_ref[tile]
            dx = spots[0:1] - own[:, 0:1]
            dy = spots[1:2] - own[:, 1:2]
            dz = spots[2:3] - own[:, 2:3]
            square = dx * dx + dy * dy + dz * dz
            scale = lax.rsqrt(square + 1.0)
            ux = dx * scale
            uy = dy * scale
            uz = dz * scale
            tx = root_fifteen * ux
            angular = [
                None,
                root_three * ux,
                root_three * uy,
                root_three * uz,
                tx * uy,
                root_fifteen * uy * uz,
                0.5 * root_five * (3.0 * uz * uz - 1.0),
                tx * uz,
                0.5 * root_fifteen * (ux * ux - uy * uy),
            ]
            for pair in range(basis // 2):
                first = times * jnp.exp2(square * rates[2 * pair])
                second = times * jnp.exp2(square * rates[2 * pair + 1])
                for degree in range(9):
                    if degree:
                        parts = [first * angular[degree], second * angular[degree]]
                    else:
                        parts = [first, second]
                    at = (degree * basis + 2 * pair) * 8
                    edge_ref[tile, at : at + 16, :] = jnp.concatenate(parts, axis=0).astype(
                        jnp.bfloat16
                    )

    def add_up(block, parity, first_row):
        edge_ref = edge_refs[block % 2]
        edges = jnp.concatenate([edge_ref[tile] for tile in range(tiles)], axis=1)
        summed = jnp.dot(edges, state_ref[parity], preferred_element_type=jnp.float32)
        for degree in range(9):
            total = summed[degree * basis * 8 : degree * basis * 8 + 8] * radial_ref[0:1, :]
            for b in range(1, basis):
                at = (degree * basis + b) * 8
                total = total + summed[at : at + 8] * radial_ref[b : b + 1, :]
            message_ref[degree, pl.ds(first_row, 8), :] = total * (1.0 / math.sqrt(NBR))

    def row_start(block):
        return pl.multiple_of(octant * slots + 8 * block, 8)

    fill_edges(0)
    add_up(blocks - 1, before, pl.multiple_of((octant * slots + atoms - 8) % atoms, 8))
    for block in range(1, blocks):
        fill_edges(block)
        add_up(block - 1, here, row_start(block - 1))

    @pl.when(octant == 7)
    def _():
        add_up(blocks - 1, here, row_start(blocks - 1))
        invariant = jnp.dot(
            message_ref[0].astype(jnp.bfloat16), mix_ref[0], preferred_element_type=jnp.float32
        )
        for degree in range(4, 9):
            tensor = jnp.dot(
                message_ref[degree].astype(jnp.bfloat16), mix_ref[2], preferred_element_type=jnp.float32
            )
            invariant = invariant + tensor * tensor
        gating = 1.0 / (1.0 + jnp.exp(-invariant))
        lifted = invariant * gating
        for own in range(8):
            at = ((1 + own // 4) * 4 + 1 + own // 2 % 2) * 4 + 1 + own % 2
            rows = slice(own * slots, (own + 1) * slots)
            next_ref[rows, :] = (packed_ref[at, :slots, :].astype(jnp.float32) + lifted[rows]).astype(
                jnp.bfloat16
            )
        weighted = gating * force_ref[...]
        for k in range(3):
            vector = jnp.dot(
                message_ref[1 + k].astype(jnp.bfloat16), mix_ref[1], preferred_element_type=jnp.float32
            )
            high, low = halves(vector * weighted)
            pushed = lax.dot_general(
                jnp.ones((8, 256), jnp.bfloat16),
                jnp.concatenate([high, low], axis=1).astype(jnp.bfloat16),
                (((1,), (1,)), ((), ())),
                preferred_element_type=jnp.float32,
            )
            push_ref[k : k + 1, :] = pushed[0:1]


def list_counts(nbr_code, own_rows):
    slots = nbr_code.shape[3]
    tiles = 28 * slots // 128
    return pl.pallas_call(
        count_kernel,
        grid=(8,),
        in_specs=[
            pl.BlockSpec((slots, NBR), lambda o: (o, 0)),
            pl.BlockSpec((slots, 4), lambda o: (o, 0)),
        ],
        out_specs=[
            pl.BlockSpec((1, tiles, slots, 128), lambda o: (o, 0, 0, 0)),
            pl.BlockSpec((slots, 128), lambda o: (o, 0)),
        ],
        out_shape=[
            jax.ShapeDtypeStruct((8, tiles, slots, 128), jnp.float32),
            jax.ShapeDtypeStruct((8 * slots, 128), jnp.float32),
        ],
        cost_estimate=pl.CostEstimate(
            flops=2_000_000_000, bytes_accessed=1_300_000, transcendentals=0
        ),
    )(nbr_code.reshape(8 * slots, NBR), own_rows)


def neighbour_sums(packed, counts, chosen, own_rows, radial_weight, mix_weight, force_weight):
    tiles, slots = counts.shape[1:3]
    channels = packed.shape[-1]
    basis = radial_weight.shape[0]
    columns = 28 * slots
    sizes = (lax.axis_size("dx"), lax.axis_size("dy"), lax.axis_size("dz"), slots, basis)
    edges = pltpu.VMEM((tiles, 9 * basis * 8, 128), jnp.bfloat16)
    whole = lambda *shape: pl.BlockSpec(shape, lambda o: (0,) * len(shape))
    return pl.pallas_call(
        functools.partial(neighbour_kernel, sizes),
        grid=(8,),
        in_specs=[
            whole(64, slots + 16, channels),
            pl.BlockSpec((1, tiles, slots, 128), lambda o: (o, 0, 0, 0)),
            pl.BlockSpec((slots, 128), lambda o: (o, 0)),
            pl.BlockSpec((slots, 4), lambda o: (o, 0)),
            whole(basis, channels),
            whole(3, channels, channels),
            whole(1, channels),
        ],
        out_specs=[whole(8 * slots, channels), whole(3, 8 * slots)],
        out_shape=[
            jax.ShapeDtypeStruct((8 * slots, channels), jnp.bfloat16),
            jax.ShapeDtypeStruct((3, 8 * slots), jnp.float32),
        ],
        scratch_shapes=[
            pltpu.VMEM((64, 8, 128), jnp.float32),
            pltpu.VMEM((2, columns, channels), jnp.bfloat16),
            pltpu.VMEM((tiles, 8, 128), jnp.float32),
            pltpu.VMEM((9, 8 * slots, channels), jnp.float32),
            edges,
            edges,
        ],
        cost_estimate=pl.CostEstimate(
            flops=8_000_000_000, bytes_accessed=2_000_000, transcendentals=2_000_000
        ),
    )(
        packed.reshape(64, slots + 16, channels),
        counts,
        chosen,
        own_rows,
        radial_weight,
        mix_weight,
        force_weight[None],
    )


def spline_rows(fraction):
    remainder = 1.0 - fraction
    square = fraction * fraction
    cube = square * fraction
    weights = [
        remainder * remainder * remainder / 6.0,
        (3.0 * cube - 6.0 * square + 4.0) / 6.0,
        (-3.0 * cube + 3.0 * square + 3.0 * fraction + 1.0) / 6.0,
        cube / 6.0,
    ]
    slopes = [
        -0.5 * remainder * remainder,
        1.5 * square - 2.0 * fraction,
        -1.5 * square + fraction + 0.5,
        0.5 * square,
    ]
    return weights, slopes


def turn(table_ref, steps, extent):
    parts = -(-extent // 128)

    def look(index):
        if extent & (extent - 1):
            index = index % extent
        else:
            index = index & (extent - 1)
        _, width = index.shape
        found = []
        for start in range(0, width, 128):
            piece = index[:, start : start + 128]
            result = None
            for part in range(parts):
                line = jnp.broadcast_to(table_ref[part : part + 1, :], piece.shape)
                lane = piece & 127 if parts > 1 else piece
                here = jnp.take_along_axis(line, lane, axis=1)
                result = here if result is None else jnp.where(piece >> 7 == part, here, result)
            found.append(result)
        return jnp.concatenate(found, axis=1) if len(found) > 1 else found[0]

    return look(steps), look(steps + 3 * extent // 4)


def wave_factors(table_ref, modes, base_row, extent):
    rows = modes.shape[0]
    width = base_row.shape[1]
    wide = jnp.broadcast_to(modes[:, :1], (rows, width))
    first = turn(table_ref, wide * base_row, extent)
    steps = [turn(table_ref, modes * t, extent) for t in (1, 2, 3)]
    steps = [tuple(jnp.concatenate([p] * (width // 128), axis=1) for p in pair) for pair in steps]
    return first, steps


def wave_of(factors, coeff):
    (cos_first, sin_first), steps = factors
    part_re = coeff[0] + coeff[1] * steps[0][0] + coeff[2] * steps[1][0] + coeff[3] * steps[2][0]
    part_im = coeff[1] * steps[0][1] + coeff[2] * steps[1][1] + coeff[3] * steps[2][1]
    return cos_first * part_re - sin_first * part_im, sin_first * part_re + cos_first * part_im


def cell_rows(coeff, local_row, cells):
    row_of = lax.broadcasted_iota(jnp.int32, (cells, local_row.shape[1]), 0)
    away = row_of - local_row
    table = jnp.where(away == 3, coeff[3], 0.0)
    for stencil in (2, 1, 0):
        table = jnp.where(away == stencil, coeff[stencil], table)
    return table


def halves(values):
    high = values.astype(jnp.bfloat16).astype(jnp.float32)
    return high, values - high


def wave_start():
    return lax.axis_index("dy") * lax.axis_size("dz") + lax.axis_index("dz")


def spread_kernel(sizes, atoms_ref, table_y_ref, table_z_ref, sums_ref):
    length_y, length_z, waves, cells = sizes
    groups, _, _ = atoms_ref.shape
    modes_y = wave_start() * waves + lax.broadcasted_iota(jnp.int32, (waves, 128), 0)
    modes_z = 1 + lax.broadcasted_iota(jnp.int32, (KZW, 128), 0)
    anchor = lax.axis_index("dx") * MB
    total = jnp.zeros(sums_ref.shape[1:], jnp.float32)
    for group in range(groups):
        chunk = atoms_ref[group]
        base = chunk[1:4].astype(jnp.int32)
        weights, _ = spline_rows(chunk[4:7])
        row = lambda d: [w[d : d + 1] for w in weights]
        y_re, y_im = wave_of(wave_factors(table_y_ref, modes_y, base[1:2], length_y), row(1))
        z_re, z_im = wave_of(wave_factors(table_z_ref, modes_z, base[2:3], length_z), row(2))
        mixed_re = []
        mixed_im = []
        for k in range(waves):
            k_re = y_re[k : k + 1]
            k_im = y_im[k : k + 1]
            mixed_re.append(k_re * z_re - k_im * z_im)
            mixed_im.append(-(k_re * z_im + k_im * z_re))
        mixed = jnp.concatenate(mixed_re + mixed_im, axis=0)
        table = cell_rows(row(0), base[0:1] - anchor, cells) * chunk[0:1]
        table_high, table_low = halves(table)
        mixed_high, mixed_low = halves(mixed)
        both = jnp.concatenate([table_high, table_low], axis=0).astype(jnp.bfloat16)
        main = lax.dot_general(
            both,
            mixed_high.astype(jnp.bfloat16),
            (((1,), (1,)), ((), ())),
            preferred_element_type=jnp.float32,
        )
        side = lax.dot_general(
            table_high.astype(jnp.bfloat16),
            mixed_low.astype(jnp.bfloat16),
            (((1,), (1,)), ((), ())),
            preferred_element_type=jnp.float32,
        )
        total = total + (main[:cells] + (main[cells:] + side))
    for copy in range(sums_ref.shape[0]):
        sums_ref[copy] = total


def push_kernel(
    sizes, atoms_ref, sums_ref, forward_ref, back_ref, table_y_ref, table_z_ref, force_ref
):
    length_x, length_y, length_z, waves, cells = sizes
    groups, _, width = atoms_ref.shape
    modes = waves * KZW
    start = wave_start() * waves
    modes_y = start + lax.broadcasted_iota(jnp.int32, (waves, 128), 0)
    modes_z = 1 + lax.broadcasted_iota(jnp.int32, (KZW, 128), 0)
    anchor = lax.axis_index("dx") * MB

    turned = jnp.dot(
        forward_ref[...], sums_ref[...], precision=highest, preferred_element_type=jnp.float32
    )
    cosine = turned[:length_x]
    sine = turned[length_x:]

    def folded(number, extent):
        number = jnp.where(2 * number >= extent, number - extent, number)
        return number.astype(jnp.float32) / (cell_size * extent)

    mode_shape = (length_x, modes)
    mode_x = lax.broadcasted_iota(jnp.int32, mode_shape, 0)
    mode_lane = lax.broadcasted_iota(jnp.int32, mode_shape, 1)
    wave_square = (
        jnp.square(folded(mode_x, length_x))
        + jnp.square(folded(start + mode_lane // KZW, length_y))
        + jnp.square(folded(mode_lane % KZW + 1, length_z))
    )
    volume = cell_size**3 * length_x * length_y * length_z
    green = (
        coulomb
        / (math.pi * volume)
        * jnp.exp(-(math.pi**2) * wave_square / ewald_beta**2)
        / wave_square
    )
    scaled = jnp.concatenate(
        [
            green * (cosine[:, :modes] + sine[:, modes:]),
            green * (cosine[:, modes:] - sine[:, :modes]),
        ],
        axis=1,
    )
    lines = back_ref[pl.ds(pl.multiple_of(lax.axis_index("dx") * cells, 8), cells), :]
    lines = jnp.concatenate([lines[:, :length_x], lines[:, length_x:]], axis=0)
    turned = jnp.dot(lines, scaled, precision=highest, preferred_element_type=jnp.float32)
    cosine = turned[:cells]
    sine = turned[cells:]
    back = jnp.concatenate(
        [cosine[:, :modes] - sine[:, modes:], sine[:, :modes] + cosine[:, modes:]], axis=1
    )
    back_high, back_low = halves(back)
    spare = jnp.zeros((128 - 3 * cells, 2 * modes), jnp.float32)
    stacked = jnp.concatenate([back_high, back_high, back_low, spare], axis=0)
    stacked = jnp.transpose(stacked).astype(jnp.bfloat16)

    for group in range(groups):
        chunk = atoms_ref[group]
        base = chunk[1:4].astype(jnp.int32)
        weights, slopes = spline_rows(chunk[4:7])
        row = lambda d: [w[d : d + 1] for w in weights]
        tilt = lambda d: [w[d : d + 1] for w in slopes]
        factors_y = wave_factors(table_y_ref, modes_y, base[1:2], length_y)
        factors_z = wave_factors(table_z_ref, modes_z, base[2:3], length_z)
        y_re, y_im = wave_of(factors_y, row(1))
        dy_re, dy_im = wave_of(factors_y, tilt(1))
        z_re, z_im = wave_of(factors_z, row(2))
        dz_re, dz_im = wave_of(factors_z, tilt(2))

        def on_atoms(coeff):
            high, low = halves(cell_rows(coeff, base[0:1] - anchor, cells))
            none = jnp.zeros((128 - 3 * cells, width), jnp.float32)
            right = jnp.concatenate([high, low, high, none], axis=0).astype(jnp.bfloat16)
            return jnp.dot(stacked, right, preferred_element_type=jnp.float32)

        value = on_atoms(row(0))
        slant = on_atoms(tilt(0))

        def along(field, wave_re, wave_im):
            sum_re = jnp.zeros((KZW, width), jnp.float32)
            sum_im = jnp.zeros((KZW, width), jnp.float32)
            for k in range(waves):
                f_re = field[k * KZW : (k + 1) * KZW]
                f_im = field[modes + k * KZW : modes + (k + 1) * KZW]
                k_re = wave_re[k : k + 1]
                k_im = wave_im[k : k + 1]
                sum_re = sum_re + (f_re * k_re - f_im * k_im)
                sum_im = sum_im + (f_re * k_im + f_im * k_re)
            return sum_re, sum_im

        def ended(pair, wave_re, wave_im):
            return 2.0 * jnp.sum(pair[0] * wave_re - pair[1] * wave_im, axis=0, keepdims=True)

        push_x = ended(along(slant, y_re, y_im), z_re, z_im)
        push_y = ended(along(value, dy_re, dy_im), z_re, z_im)
        push_z = ended(along(value, y_re, y_im), dz_re, dz_im)
        force_ref[group] = jnp.concatenate([push_x, push_y, push_z], axis=0) * (
            -chunk[0:1] / cell_size
        )


def cosine_period(extent):
    lines = -(-extent // 128)
    steps = np.arange(lines * 128).reshape(lines, 128)
    return jnp.asarray(np.cos(2.0 * np.pi * steps / extent).astype(np.float32))


def long_range(mesh_base, mesh_frac, charge, counts):
    count_x = lax.axis_size("dx")
    count_y = lax.axis_size("dy")
    count_z = lax.axis_size("dz")
    atom_total = charge.size
    groups = count_y * count_z
    cells = -(-(MB + 3) // 8) * 8
    length_x = MB * count_x
    length_y = MB * count_y
    length_z = MB * count_z
    waves = MB // count_z
    modes = waves * KZW
    packed = jnp.concatenate(
        [
            charge.reshape(1, atom_total),
            mesh_base.reshape(3, atom_total).astype(jnp.float32),
            mesh_frac.reshape(3, atom_total),
        ],
        axis=0,
    )
    packed = jnp.broadcast_to(packed[None], (groups, 7, atom_total))
    atoms = lax.all_to_all(packed, ("dy", "dz"), 0, 0, tiled=True)
    table_y = cosine_period(length_y)
    table_z = cosine_period(length_z)
    sums = pl.pallas_call(
        functools.partial(spread_kernel, (length_y, length_z, waves, cells)),
        out_shape=jax.ShapeDtypeStruct((count_x, cells, 2 * modes), jnp.float32),
    )(atoms, table_y, table_z)
    received = lax.all_to_all(sums, "dx", 0, 0, tiled=True)
    received = received.reshape(count_x * cells, 2 * modes)
    received, counts = lax.optimization_barrier((received, counts))
    places = (np.arange(count_x) * MB)[:, None] + np.arange(cells)[None, :]
    angles = 2.0 * np.pi / length_x * (np.arange(length_x)[:, None] * places.reshape(1, -1) % length_x)
    forward = np.concatenate([np.cos(angles), np.sin(angles)], axis=0).astype(np.float32)
    parts = pl.pallas_call(
        functools.partial(push_kernel, (length_x, length_y, length_z, waves, cells)),
        out_shape=jax.ShapeDtypeStruct((groups, 3, atom_total), jnp.float32),
    )(atoms, received, jnp.asarray(forward), jnp.asarray(forward.T.copy()), table_y, table_z)
    parts = lax.all_to_all(parts, ("dy", "dz"), 0, 0, tiled=True)
    return jnp.sum(parts, axis=0), counts


def shards(
    node_state,
    mesh_base,
    mesh_frac,
    charge,
    nbr_code,
    nbr_count,
    radial_weight,
    mix_weight,
    force_weight,
):
    octants = node_state.shape[3]
    atom_total = 8 * octants
    places = mesh_base.astype(jnp.float32) + mesh_frac
    own_rows = jnp.transpose(
        jnp.concatenate([places, nbr_count.astype(jnp.float32)[None]], axis=0).reshape(4, atom_total)
    )
    counts, chosen = list_counts(nbr_code, own_rows)
    long_force, counts = long_range(mesh_base, mesh_frac, charge, counts)
    packed_halo = spread_halo(pack_atoms(node_state, places), 1)
    updated, short_force = neighbour_sums(
        packed_halo, counts, chosen, own_rows, radial_weight, mix_weight, force_weight
    )
    node_next = updated.reshape(node_state.shape)
    forces = (short_force + long_force).reshape(3, 2, 2, 2, octants)
    return (node_next, forces)


def solution(mesh):
    placed = (
        P("dx", "dy", "dz", None, None),
        P(None, "dx", "dy", "dz", None),
        P(None, "dx", "dy", "dz", None),
        P("dx", "dy", "dz", None),
        P("dx", "dy", "dz", None, None),
        P("dx", "dy", "dz", None),
        P(),
        P(),
        P(),
    )

    return jax.shard_map(
        shards,
        mesh=mesh,
        in_specs=placed,
        out_specs=(P("dx", "dy", "dz", None, None), P(None, "dx", "dy", "dz", None)),
        check_vma=False,
    )
```

```python
import functools
import math

import jax
import jax.numpy as jnp
from jax import lax
from jax.experimental import pallas as pl
from jax.experimental.pallas import tpu as pltpu
from jax.sharding import PartitionSpec as P


NBR = 128
MB = 32
KZW = 8


cell_size = 1.13
ewald_beta = 0.625
coulomb = 332.0637
sigma_low = 8.0
sigma_rate = 1.5
highest = lax.Precision.HIGHEST


def neighbours_along(block, axis, dim):
    count = lax.axis_size(axis)
    if count == 2:
        other = lax.ppermute(block, axis, [(0, 1), (1, 0)])
        return other, other
    head = lax.slice_in_dim(block, 0, 1, axis=dim)
    tail = lax.slice_in_dim(block, block.shape[dim] - 1, block.shape[dim], axis=dim)
    below = lax.ppermute(tail, axis, [(i, (i + 1) % count) for i in range(count)])
    above = lax.ppermute(head, axis, [((i + 1) % count, i) for i in range(count)])
    return below, above


def spread_halo(block):
    for axis, dim in (("dx", 0), ("dy", 1)):
        below, above = neighbours_along(block, axis, dim)
        below = lax.slice_in_dim(below, below.shape[dim] - 1, below.shape[dim], axis=dim)
        above = lax.slice_in_dim(above, 0, 1, axis=dim)
        block = jnp.concatenate([below, block, above], axis=dim)
    return (block,) + neighbours_along(block, "dz", 2)


def pack_kernel(*refs):
    sources, held, fetched = refs[:7], refs[11:18], refs[18]
    atoms_ref, block_ref, own_ref, channel_ref = refs[7:11]
    copies = [
        pltpu.make_async_copy(source, here, fetched.at[at])
        for at, (source, here) in enumerate(zip(sources, held))
    ]
    for copy in copies:
        copy.start()
    for copy in copies:
        copy.wait()
    state_ref, base_ref, frac_ref, charge_ref, live_ref, radial_ref, force_ref = held
    channel_ref[...] = jnp.concatenate([radial_ref[...], force_ref[...]], axis=0)
    slots = state_ref.shape[3]
    sevens = []
    fours = []
    for octant in range(8):
        at = (octant // 4, octant // 2 % 2, slice(octant % 2, octant % 2 + 1))
        charge = charge_ref[at]
        base = jnp.concatenate([base_ref[(d,) + at] for d in range(3)], axis=0).astype(jnp.float32)
        frac = jnp.concatenate([frac_ref[(d,) + at] for d in range(3)], axis=0)
        places = base + frac
        sevens.append(jnp.concatenate([charge, base, frac], axis=0))
        fours.append(jnp.concatenate([places, live_ref[at].astype(jnp.float32)], axis=0))
        pieces = []
        rest = places
        for _ in range(3):
            piece = rest.astype(jnp.bfloat16).astype(jnp.float32)
            pieces.append(piece)
            rest = rest - piece
        pieces.append(jnp.zeros((3, 128 - 3 * slots), jnp.float32))
        cells = jnp.concatenate(pieces, axis=1)
        cells = jnp.concatenate([cells, jnp.zeros((13, 128), jnp.float32)], axis=0)
        block_ref[octant, slots:, :] = cells.astype(jnp.bfloat16)
        block_ref[octant, :slots, :] = state_ref[octant // 4, octant // 2 % 2, octant % 2]
    seven = jnp.concatenate(sevens, axis=1)
    for copy in range(atoms_ref.shape[0]):
        atoms_ref[copy] = seven
    four = jnp.concatenate(fours, axis=1)
    four = jnp.concatenate([four, jnp.zeros_like(four)], axis=0)
    own_ref[...] = jnp.transpose(four)


def pack_atoms(node_state, mesh_base, mesh_frac, charge, nbr_count, radial_weight, force_weight):
    slots, channels = node_state.shape[3:]
    groups = lax.axis_size("dy") * lax.axis_size("dz")
    arrays = (
        node_state,
        mesh_base,
        mesh_frac,
        charge,
        nbr_count,
        radial_weight,
        force_weight[None],
    )
    atoms, block, own_rows, channel_rows = pl.pallas_call(
        pack_kernel,
        out_shape=[
            jax.ShapeDtypeStruct((groups, 7, 8 * slots), jnp.float32),
            jax.ShapeDtypeStruct((8, slots + 16, channels), jnp.bfloat16),
            jax.ShapeDtypeStruct((8 * slots, 8), jnp.float32),
            jax.ShapeDtypeStruct((radial_weight.shape[0] + 1, channels), jnp.float32),
        ],
        in_specs=[pl.BlockSpec(memory_space=pltpu.HBM)] * len(arrays),
        scratch_shapes=[pltpu.VMEM(array.shape, array.dtype) for array in arrays]
        + [pltpu.SemaphoreType.DMA((len(arrays),))],
        compiler_params=pltpu.CompilerParams(vmem_limit_bytes=4 << 20),
    )(*[pltpu.with_memory_space_constraint(array, pltpu.HBM) for array in arrays])
    block = block.reshape(2, 2, 2, slots + 16, channels)
    return atoms, block, own_rows, channel_rows


def count_kernel(code_ref, own_ref, *refs):
    count_ref, chosen_ref = refs[-2:]
    octants, tiles, slots, _ = count_ref.shape
    row_of = lax.broadcasted_iota(jnp.int32, (8, 128), 0)
    lane_of = lax.broadcasted_iota(jnp.int32, (8, 128), 1)
    cell_iota = lax.broadcasted_iota(jnp.int32, (128, 128), 0).astype(jnp.float32).astype(jnp.bfloat16)
    one = jnp.ones((128, 128), jnp.bfloat16)
    zero = jnp.zeros((128, 128), jnp.bfloat16)
    lane_float = lane_of.astype(jnp.float32)
    pieces = [(octant, block) for octant in range(octants) for block in range(slots // 8)]
    for octant, block in pieces:
        rows = slice(octant * slots + 8 * block, octant * slots + 8 * block + 8)
        codes = code_ref[rows, :]
        live = lane_float < own_ref[rows, 3:4]
        high = jnp.where(live, codes >> 7, 64)
        low = (codes & 127).astype(jnp.float32)
        for atom in range(8):
            low_row = jnp.broadcast_to(low[atom : atom + 1], (16, 128)).astype(jnp.bfloat16)
            low_hot = jnp.where(cell_iota == jnp.concatenate([low_row] * 8, axis=0), one, zero)
            high_hot = (row_of == high[atom : atom + 1]).astype(jnp.float32).astype(jnp.bfloat16)
            counted = lax.dot_general(
                high_hot, low_hot, (((1,), (1,)), ((), ())), preferred_element_type=jnp.float32
            )
            count_ref[octant, :, 8 * block + atom, :] = counted[:tiles]
    for octant, block in pieces:
        own = slice(8 * block, 8 * block + 8)
        best = jnp.full((8, 128), -1.0, jnp.float32)
        for tile in range(tiles):
            times = count_ref[octant, tile, own, :]
            split = (times == 3.0) | ((times > 4.0) & (times < 8.0))
            best = jnp.where(split, lane_float + 128.0 * tile, best)
        chosen = jnp.max(best, axis=1, keepdims=True)
        rows = slice(octant * slots + 8 * block, octant * slots + 8 * block + 8)
        chosen_ref[rows, :] = jnp.broadcast_to(chosen, (8, 128))
        rest = jnp.zeros((8, 128), jnp.float32)
        for tile in range(tiles):
            times = count_ref[octant, tile, own, :]
            hot = lane_float + 128.0 * tile == chosen
            part = jnp.where(times > 4.0, times - 4.0, times - 2.0)
            rest = rest + jnp.where(hot, part, 0.0)
            count_ref[octant, tile, own, :] = jnp.where(hot, times - part, times)
        total = jnp.sum(rest, axis=1, keepdims=True)
        spare = lane_of - (128 - slots) == row_of + 8 * block
        last = count_ref[octant, tiles - 1, own, :]
        count_ref[octant, tiles - 1, own, :] = jnp.where(spare, total, last)


def neighbour_kernel(
    sizes,
    block_ref,
    below_ref,
    above_ref,
    count_ref,
    chosen_ref,
    own_ref,
    radial_ref,
    mix_ref,
    next_ref,
    push_ref,
    halo_ref,
    place_ref,
    state_ref,
    table_ref,
    message_ref,
    *edge_refs,
):
    count_x, count_y, count_z, slots, basis = sizes
    octant = pl.program_id(0)
    columns = state_ref.shape[1]
    tiles = columns // 128
    per_tile = 128 // slots
    blocks = slots // 8
    atoms = 8 * slots
    corner = ((octant // 4) * 4 + octant // 2 % 2) * 4 + octant % 2
    sides = [(side // 9 * 4 + side // 3 % 3) * 4 + side % 3 for side in range(27)]
    row_of = lax.broadcasted_iota(jnp.int32, (8, 128), 0)
    lane_of = lax.broadcasted_iota(jnp.int32, (8, 128), 1)
    lane_float = lane_of.astype(jnp.float32)
    here = octant % 2
    before = 1 - here

    @pl.when(octant == 0)
    def _():
        half = MB // 2
        for parity in range(2):
            state_ref[parity, 27 * slots :, :] = jnp.zeros((slots, 128), jnp.bfloat16)
        starts = [2 * lax.axis_index(axis) - 1 for axis in ("dx", "dy", "dz")]

        def unwrapped(place, start, count):
            reach = start + place
            below = jnp.where(reach < 0, -2 * count * half, 0)
            return jnp.where(reach >= 2 * count, 2 * count * half, below).astype(jnp.float32)

        @pl.loop(0, 16, unroll=2)
        def _(column):
            shift_x = unwrapped(column // 4, starts[0], count_x)
            shift_y = unwrapped(column % 4, starts[1], count_y)
            for level in range(4):
                if level == 0:
                    source = below_ref.at[column, below_ref.shape[1] - 1]
                elif level == 3:
                    source = above_ref.at[column, 0]
                else:
                    source = block_ref.at[column, level - 1]
                cell = column * 4 + level
                halo_ref[cell] = source[:slots, :]
                rows = source[slots:, :].astype(jnp.float32)[:8]
                total = rows + pltpu.roll(rows, 128 - slots, 1)
                total = total + pltpu.roll(rows, 128 - 2 * slots, 1)
                shift_z = unwrapped(level, starts[2], count_z)
                shift = jnp.where(row_of == 0, shift_x, jnp.where(row_of == 1, shift_y, shift_z))
                place_ref[cell] = total + shift

    for side in range(27):
        state_ref[here, side * slots : (side + 1) * slots, :] = halo_ref[corner + sides[side]]
    for tile in range(tiles):
        joined = jnp.zeros((8, 128), jnp.float32)
        for part in range(per_tile):
            side = tile * per_tile + part
            if side < 27:
                moved = place_ref[corner + sides[side]]
                if part:
                    moved = pltpu.roll(moved, part * slots, 1)
                joined = jnp.where(lane_of // slots == part, moved, joined)
        table_ref[tile] = joined

    chosen = chosen_ref[...]
    wide_lane = lax.broadcasted_iota(jnp.int32, (slots, 128), 1).astype(jnp.float32)
    hots = jnp.concatenate(
        [jnp.where(wide_lane + 128.0 * tile == chosen, 1.0, 0.0) for tile in range(tiles)], axis=1
    ).astype(jnp.bfloat16)
    state_ref[here, 27 * slots :, :] = jnp.dot(
        hots, state_ref[here], preferred_element_type=jnp.float32
    ).astype(jnp.bfloat16)
    pieces = []
    spots = jnp.concatenate([table_ref[tile] for tile in range(tiles)], axis=1)
    for _ in range(3):
        piece = spots.astype(jnp.bfloat16).astype(jnp.float32)
        pieces.append(piece)
        spots = spots - piece
    pieces = jnp.concatenate(pieces + [jnp.zeros_like(spots)], axis=0).astype(jnp.bfloat16)
    found = lax.dot_general(
        pieces, hots, (((1,), (1,)), ((), ())), preferred_element_type=jnp.float32
    )
    found = (found[:8] + found[8:16]) + found[16:24]
    table_ref[tiles - 1] = jnp.where(
        lane_of < 128 - slots, table_ref[tiles - 1], jnp.concatenate([found] * per_tile, axis=1)
    )

    root_three = math.sqrt(3.0)
    root_fifteen = math.sqrt(15.0)
    root_five = math.sqrt(5.0)
    rates = [
        -(cell_size**2) / (sigma_low * sigma_rate**b) ** 2 * math.log2(math.e) for b in range(basis)
    ]

    def fill_edges(block):
        rows = slice(8 * block, 8 * block + 8)
        edge_ref = edge_refs[block % 2]
        own = own_ref[rows, :]
        for tile in range(tiles):
            times = count_ref[0, tile, rows, :]
            spots = table_ref[tile]
            dx = spots[0:1] - own[:, 0:1]
            dy = spots[1:2] - own[:, 1:2]
            dz = spots[2:3] - own[:, 2:3]
            square = dx * dx + dy * dy + dz * dz
            scale = lax.rsqrt(square + 1.0)
            ux = dx * scale
            uy = dy * scale
            uz = dz * scale
            tx = root_fifteen * ux
            angular = [
                None,
                root_three * ux,
                root_three * uy,
                root_three * uz,
                tx * uy,
                root_fifteen * uy * uz,
                0.5 * root_five * (3.0 * uz * uz - 1.0),
                tx * uz,
                0.5 * root_fifteen * (ux * ux - uy * uy),
            ]
            for pair in range(basis // 2):
                first = times * jnp.exp2(square * rates[2 * pair])
                second = times * jnp.exp2(square * rates[2 * pair + 1])
                for degree in range(9):
                    if degree:
                        parts = [first * angular[degree], second * angular[degree]]
                    else:
                        parts = [first, second]
                    at = (degree * basis + 2 * pair) * 8
                    edge_ref[tile, at : at + 16, :] = jnp.concatenate(parts, axis=0).astype(
                        jnp.bfloat16
                    )

    def add_up(block, parity, first_row):
        edge_ref = edge_refs[block % 2]
        edges = jnp.concatenate([edge_ref[tile] for tile in range(tiles)], axis=1)
        summed = jnp.dot(edges, state_ref[parity], preferred_element_type=jnp.float32)
        for degree in range(9):
            total = summed[degree * basis * 8 : degree * basis * 8 + 8] * radial_ref[0:1, :]
            for b in range(1, basis):
                at = (degree * basis + b) * 8
                total = total + summed[at : at + 8] * radial_ref[b : b + 1, :]
            message_ref[degree, pl.ds(first_row, 8), :] = total * (1.0 / math.sqrt(NBR))

    def row_start(block):
        return pl.multiple_of(octant * slots + 8 * block, 8)

    fill_edges(0)
    add_up(blocks - 1, before, pl.multiple_of((octant * slots + atoms - 8) % atoms, 8))
    for block in range(1, blocks):
        fill_edges(block)
        add_up(block - 1, here, row_start(block - 1))

    @pl.when(octant == 7)
    def _():
        add_up(blocks - 1, here, row_start(blocks - 1))
        invariant = jnp.dot(
            message_ref[0].astype(jnp.bfloat16), mix_ref[0], preferred_element_type=jnp.float32
        )
        for degree in range(4, 9):
            tensor = jnp.dot(
                message_ref[degree].astype(jnp.bfloat16), mix_ref[2], preferred_element_type=jnp.float32
            )
            invariant = invariant + tensor * tensor
        gating = 1.0 / (1.0 + jnp.exp(-invariant))
        lifted = invariant * gating
        for own in range(8):
            at = ((1 + own // 4) * 4 + 1 + own // 2 % 2) * 4 + 1 + own % 2
            rows = slice(own * slots, (own + 1) * slots)
            next_ref[rows, :] = (halo_ref[at].astype(jnp.float32) + lifted[rows]).astype(jnp.bfloat16)
        weighted = gating * radial_ref[basis : basis + 1, :]
        for k in range(3):
            vector = jnp.dot(
                message_ref[1 + k].astype(jnp.bfloat16), mix_ref[1], preferred_element_type=jnp.float32
            )
            high, low = halves(vector * weighted)
            pushed = lax.dot_general(
                jnp.ones((8, 256), jnp.bfloat16),
                jnp.concatenate([high, low], axis=1).astype(jnp.bfloat16),
                (((1,), (1,)), ((), ())),
                preferred_element_type=jnp.float32,
            )
            push_ref[k : k + 1, :] = pushed[0:1]


def list_counts(nbr_code, own_rows, first, earlier):
    slots = nbr_code.shape[3]
    tiles = 28 * slots // 128
    together = 2
    start = first // together
    return pl.pallas_call(
        count_kernel,
        grid=(4 // together,),
        in_specs=[
            pl.BlockSpec((together * slots, NBR), lambda o: (o + start, 0)),
            pl.BlockSpec((together * slots, 8), lambda o: (o + start, 0)),
        ]
        + [pl.BlockSpec(memory_space=pl.ANY)] * len(earlier),
        out_specs=[
            pl.BlockSpec((together, tiles, slots, 128), lambda o: (o + start, 0, 0, 0)),
            pl.BlockSpec((together * slots, 128), lambda o: (o + start, 0)),
        ],
        out_shape=[
            jax.ShapeDtypeStruct((8, tiles, slots, 128), jnp.float32),
            jax.ShapeDtypeStruct((8 * slots, 128), jnp.float32),
        ],
        input_output_aliases={2: 0, 3: 1} if earlier else {},
        cost_estimate=pl.CostEstimate(
            flops=1_000_000_000, bytes_accessed=700_000, transcendentals=0
        ),
        compiler_params=pltpu.CompilerParams(vmem_limit_bytes=6 << 20),
    )(nbr_code.reshape(8 * slots, NBR), own_rows, *earlier)


def neighbour_sums(packed, counts, chosen, own_rows, channel_rows, mix_weight):
    tiles, slots = counts.shape[1:3]
    channels = packed[0].shape[-1]
    packed = [block.reshape((16, -1) + block.shape[3:]) for block in packed]
    basis = channel_rows.shape[0] - 1
    columns = 28 * slots
    sizes = (lax.axis_size("dx"), lax.axis_size("dy"), lax.axis_size("dz"), slots, basis)
    edges = pltpu.VMEM((tiles, 9 * basis * 8, 128), jnp.bfloat16)
    whole = lambda *shape: pl.BlockSpec(shape, lambda o: (0,) * len(shape))
    return pl.pallas_call(
        functools.partial(neighbour_kernel, sizes),
        grid=(8,),
        in_specs=[
            *[whole(*block.shape) for block in packed],
            pl.BlockSpec((1, tiles, slots, 128), lambda o: (o, 0, 0, 0)),
            pl.BlockSpec((slots, 128), lambda o: (o, 0)),
            pl.BlockSpec((slots, 8), lambda o: (o, 0)),
            whole(basis + 1, channels),
            whole(3, channels, channels),
        ],
        out_specs=[whole(8 * slots, channels), whole(3, 8 * slots)],
        out_shape=[
            jax.ShapeDtypeStruct((8 * slots, channels), jnp.bfloat16),
            jax.ShapeDtypeStruct((3, 8 * slots), jnp.float32),
        ],
        scratch_shapes=[
            pltpu.VMEM((64, slots, channels), jnp.bfloat16),
            pltpu.VMEM((64, 8, 128), jnp.float32),
            pltpu.VMEM((2, columns, channels), jnp.bfloat16),
            pltpu.VMEM((tiles, 8, 128), jnp.float32),
            pltpu.VMEM((9, 8 * slots, channels), jnp.float32),
            edges,
            edges,
        ],
        compiler_params=pltpu.CompilerParams(vmem_limit_bytes=16 << 20),
        cost_estimate=pl.CostEstimate(
            flops=8_000_000_000, bytes_accessed=2_000_000, transcendentals=2_000_000
        ),
    )(
        *packed,
        counts,
        chosen,
        own_rows,
        channel_rows,
        mix_weight,
    )


def spline_rows(fraction):
    remainder = 1.0 - fraction
    square = fraction * fraction
    cube = square * fraction
    weights = [
        remainder * remainder * remainder / 6.0,
        (3.0 * cube - 6.0 * square + 4.0) / 6.0,
        (-3.0 * cube + 3.0 * square + 3.0 * fraction + 1.0) / 6.0,
        cube / 6.0,
    ]
    slopes = [
        -0.5 * remainder * remainder,
        1.5 * square - 2.0 * fraction,
        -1.5 * square + fraction + 0.5,
        0.5 * square,
    ]
    return weights, slopes


def turn(steps, extent):
    _, width = steps.shape
    parts = -(-extent // 128)
    lane = lax.broadcasted_iota(jnp.int32, (8, 128), 1)
    lines = [
        jnp.cos((lane + 128 * part).astype(jnp.float32) * (2.0 * math.pi / extent))[:1]
        for part in range(parts)
    ]

    def look(index):
        if extent & (extent - 1):
            index = index % extent
        else:
            index = index & (extent - 1)
        found = []
        for start in range(0, width, 128):
            piece = index[:, start : start + 128]
            result = None
            for part in range(parts):
                line = jnp.broadcast_to(lines[part], piece.shape)
                at = piece & 127 if parts > 1 else piece
                here = jnp.take_along_axis(line, at, axis=1)
                result = here if result is None else jnp.where(piece >> 7 == part, here, result)
            found.append(result)
        return jnp.concatenate(found, axis=1) if len(found) > 1 else found[0]

    return look(steps), look(steps + 3 * extent // 4)


def wave_factors(modes, base_row, extent):
    rows = modes.shape[0]
    width = base_row.shape[1]
    wide = jnp.broadcast_to(modes[:, :1], (rows, width))
    first = turn(wide * base_row, extent)
    steps = [turn(modes * t, extent) for t in (1, 2, 3)]
    steps = [tuple(jnp.concatenate([p] * (width // 128), axis=1) for p in pair) for pair in steps]
    return first, steps


def wave_of(factors, coeff):
    (cos_first, sin_first), steps = factors
    part_re = coeff[0] + coeff[1] * steps[0][0] + coeff[2] * steps[1][0] + coeff[3] * steps[2][0]
    part_im = coeff[1] * steps[0][1] + coeff[2] * steps[1][1] + coeff[3] * steps[2][1]
    return cos_first * part_re - sin_first * part_im, sin_first * part_re + cos_first * part_im


def cell_rows(coeff, local_row, cells):
    row_of = lax.broadcasted_iota(jnp.int32, (cells, local_row.shape[1]), 0)
    away = row_of - local_row
    table = jnp.where(away == 3, coeff[3], 0.0)
    for stencil in (2, 1, 0):
        table = jnp.where(away == stencil, coeff[stencil], table)
    return table


def halves(values):
    high = values.astype(jnp.bfloat16).astype(jnp.float32)
    return high, values - high


def wave_start():
    return lax.axis_index("dy") * lax.axis_size("dz") + lax.axis_index("dz")


def spread_kernel(sizes, atoms_ref, sums_ref):
    length_y, length_z, waves, cells = sizes
    groups, _, _ = atoms_ref.shape
    modes_y = wave_start() * waves + lax.broadcasted_iota(jnp.int32, (waves, 128), 0)
    modes_z = 1 + lax.broadcasted_iota(jnp.int32, (KZW, 128), 0)
    anchor = lax.axis_index("dx") * MB
    total = jnp.zeros(sums_ref.shape[1:], jnp.float32)
    for group in range(groups):
        chunk = atoms_ref[group]
        base = chunk[1:4].astype(jnp.int32)
        weights, _ = spline_rows(chunk[4:7])
        row = lambda d: [w[d : d + 1] for w in weights]
        y_re, y_im = wave_of(wave_factors(modes_y, base[1:2], length_y), row(1))
        z_re, z_im = wave_of(wave_factors(modes_z, base[2:3], length_z), row(2))
        mixed_re = []
        mixed_im = []
        for k in range(waves):
            k_re = y_re[k : k + 1]
            k_im = y_im[k : k + 1]
            mixed_re.append(k_re * z_re - k_im * z_im)
            mixed_im.append(-(k_re * z_im + k_im * z_re))
        mixed = jnp.concatenate(mixed_re + mixed_im, axis=0)
        table = cell_rows(row(0), base[0:1] - anchor, cells) * chunk[0:1]
        table_high, table_low = halves(table)
        mixed_high, mixed_low = halves(mixed)
        both = jnp.concatenate([table_high, table_low], axis=0).astype(jnp.bfloat16)
        main = lax.dot_general(
            both,
            mixed_high.astype(jnp.bfloat16),
            (((1,), (1,)), ((), ())),
            preferred_element_type=jnp.float32,
        )
        side = lax.dot_general(
            table_high.astype(jnp.bfloat16),
            mixed_low.astype(jnp.bfloat16),
            (((1,), (1,)), ((), ())),
            preferred_element_type=jnp.float32,
        )
        total = total + (main[:cells] + (main[cells:] + side))
    for copy in range(sums_ref.shape[0]):
        sums_ref[copy] = total


def push_kernel(sizes, atoms_ref, sums_ref, force_ref):
    length_x, length_y, length_z, waves, cells = sizes
    groups, _, width = atoms_ref.shape
    modes = waves * KZW
    start = wave_start() * waves
    modes_y = start + lax.broadcasted_iota(jnp.int32, (waves, 128), 0)
    modes_z = 1 + lax.broadcasted_iota(jnp.int32, (KZW, 128), 0)
    anchor = lax.axis_index("dx") * MB

    count_x = length_x // MB
    lined = -(-count_x * cells // 128) * 128
    place = lax.broadcasted_iota(jnp.int32, (1, lined), 1)
    place = place + (MB - cells) * (place // cells)
    mode = lax.broadcasted_iota(jnp.int32, (length_x, lined), 0)
    forward = jnp.concatenate(turn(mode * place, length_x), axis=0)[:, : count_x * cells]
    turned = jnp.dot(
        forward, sums_ref[...], precision=highest, preferred_element_type=jnp.float32
    )
    cosine = turned[:length_x]
    sine = turned[length_x:]

    def folded(number, extent):
        number = jnp.where(2 * number >= extent, number - extent, number)
        return number.astype(jnp.float32) / (cell_size * extent)

    mode_shape = (length_x, modes)
    mode_x = lax.broadcasted_iota(jnp.int32, mode_shape, 0)
    mode_lane = lax.broadcasted_iota(jnp.int32, mode_shape, 1)
    wave_square = (
        jnp.square(folded(mode_x, length_x))
        + jnp.square(folded(start + mode_lane // KZW, length_y))
        + jnp.square(folded(mode_lane % KZW + 1, length_z))
    )
    volume = cell_size**3 * length_x * length_y * length_z
    green = (
        coulomb
        / (math.pi * volume)
        * jnp.exp(-(math.pi**2) * wave_square / ewald_beta**2)
        / wave_square
    )
    scaled = jnp.concatenate(
        [
            green * (cosine[:, :modes] + sine[:, modes:]),
            green * (cosine[:, modes:] - sine[:, :modes]),
        ],
        axis=1,
    )
    cell = anchor + lax.broadcasted_iota(jnp.int32, (cells, length_x), 0)
    mode = lax.broadcasted_iota(jnp.int32, (cells, length_x), 1)
    lines = jnp.concatenate(turn(cell * mode, length_x), axis=0)
    turned = jnp.dot(lines, scaled, precision=highest, preferred_element_type=jnp.float32)
    cosine = turned[:cells]
    sine = turned[cells:]
    back = jnp.concatenate(
        [cosine[:, :modes] - sine[:, modes:], sine[:, :modes] + cosine[:, modes:]], axis=1
    )
    back_high, back_low = halves(back)
    spare = jnp.zeros((128 - 3 * cells, 2 * modes), jnp.float32)
    stacked = jnp.concatenate([back_high, back_high, back_low, spare], axis=0)
    stacked = jnp.transpose(stacked).astype(jnp.bfloat16)

    for group in range(groups):
        chunk = atoms_ref[group]
        base = chunk[1:4].astype(jnp.int32)
        weights, slopes = spline_rows(chunk[4:7])
        row = lambda d: [w[d : d + 1] for w in weights]
        tilt = lambda d: [w[d : d + 1] for w in slopes]
        factors_y = wave_factors(modes_y, base[1:2], length_y)
        factors_z = wave_factors(modes_z, base[2:3], length_z)
        y_re, y_im = wave_of(factors_y, row(1))
        dy_re, dy_im = wave_of(factors_y, tilt(1))
        z_re, z_im = wave_of(factors_z, row(2))
        dz_re, dz_im = wave_of(factors_z, tilt(2))

        def on_atoms(coeff):
            high, low = halves(cell_rows(coeff, base[0:1] - anchor, cells))
            none = jnp.zeros((128 - 3 * cells, width), jnp.float32)
            right = jnp.concatenate([high, low, high, none], axis=0).astype(jnp.bfloat16)
            return jnp.dot(stacked, right, preferred_element_type=jnp.float32)

        value = on_atoms(row(0))
        slant = on_atoms(tilt(0))

        def along(field, wave_re, wave_im):
            sum_re = jnp.zeros((KZW, width), jnp.float32)
            sum_im = jnp.zeros((KZW, width), jnp.float32)
            for k in range(waves):
                f_re = field[k * KZW : (k + 1) * KZW]
                f_im = field[modes + k * KZW : modes + (k + 1) * KZW]
                k_re = wave_re[k : k + 1]
                k_im = wave_im[k : k + 1]
                sum_re = sum_re + (f_re * k_re - f_im * k_im)
                sum_im = sum_im + (f_re * k_im + f_im * k_re)
            return sum_re, sum_im

        def ended(pair, wave_re, wave_im):
            return 2.0 * jnp.sum(pair[0] * wave_re - pair[1] * wave_im, axis=0, keepdims=True)

        push_x = ended(along(slant, y_re, y_im), z_re, z_im)
        push_y = ended(along(value, dy_re, dy_im), z_re, z_im)
        push_z = ended(along(value, y_re, y_im), dz_re, dz_im)
        force_ref[group] = jnp.concatenate([push_x, push_y, push_z], axis=0) * (
            -chunk[0:1] / cell_size
        )


def long_range(packed, counts):
    count_x = lax.axis_size("dx")
    count_y = lax.axis_size("dy")
    count_z = lax.axis_size("dz")
    groups, _, atom_total = packed.shape
    cells = -(-(MB + 3) // 8) * 8
    length_x = MB * count_x
    length_y = MB * count_y
    length_z = MB * count_z
    waves = MB // count_z
    modes = waves * KZW
    atoms = lax.all_to_all(packed, ("dy", "dz"), 0, 0, tiled=True)
    sums = pl.pallas_call(
        functools.partial(spread_kernel, (length_y, length_z, waves, cells)),
        out_shape=jax.ShapeDtypeStruct((count_x, cells, 2 * modes), jnp.float32),
        compiler_params=pltpu.CompilerParams(vmem_limit_bytes=8 << 20),
    )(atoms)
    received = lax.all_to_all(sums, "dx", 0, 0, tiled=True)
    received = received.reshape(count_x * cells, 2 * modes)
    received, counts = lax.optimization_barrier((received, counts))
    parts = pl.pallas_call(
        functools.partial(push_kernel, (length_x, length_y, length_z, waves, cells)),
        out_shape=jax.ShapeDtypeStruct((groups, 3, atom_total), jnp.float32),
        compiler_params=pltpu.CompilerParams(vmem_limit_bytes=16 << 20),
    )(atoms, received)
    parts = lax.all_to_all(parts, ("dy", "dz"), 0, 0, tiled=True)
    return jnp.sum(parts, axis=0), counts


def shards(
    node_state,
    mesh_base,
    mesh_frac,
    charge,
    nbr_code,
    nbr_count,
    radial_weight,
    mix_weight,
    force_weight,
):
    octants = node_state.shape[3]
    packed, block, own_rows, channel_rows = pack_atoms(
        node_state, mesh_base, mesh_frac, charge, nbr_count, radial_weight, force_weight
    )
    earlier = list_counts(nbr_code, own_rows, 0, ())
    counts, chosen = list_counts(nbr_code, own_rows, 4, earlier)
    long_force, counts = long_range(packed, counts)
    packed_halo = spread_halo(block)
    updated, short_force = neighbour_sums(
        packed_halo, counts, chosen, own_rows, channel_rows, mix_weight
    )
    node_next = updated.reshape(node_state.shape)
    forces = (short_force + long_force).reshape(3, 2, 2, 2, octants)
    return (node_next, forces)


def solution(mesh):
    placed = (
        P("dx", "dy", "dz", None, None),
        P(None, "dx", "dy", "dz", None),
        P(None, "dx", "dy", "dz", None),
        P("dx", "dy", "dz", None),
        P("dx", "dy", "dz", None, None),
        P("dx", "dy", "dz", None),
        P(),
        P(),
        P(),
    )

    return jax.shard_map(
        shards,
        mesh=mesh,
        in_specs=placed,
        out_specs=(P("dx", "dy", "dz", None, None), P(None, "dx", "dy", "dz", None)),
        check_vma=False,
    )
```

```python
import functools
import math

import jax
import jax.numpy as jnp
from jax import lax
from jax.experimental import pallas as pl
from jax.experimental.pallas import tpu as pltpu
from jax.sharding import PartitionSpec as P


NBR = 128
MB = 32
KZW = 8


cell_size = 1.13
ewald_beta = 0.625
coulomb = 332.0637
sigma_low = 8.0
sigma_rate = 1.5
highest = lax.Precision.HIGHEST


def neighbours_along(block, axis, dim):
    count = lax.axis_size(axis)
    if count == 2:
        other = lax.ppermute(block, axis, [(0, 1), (1, 0)])
        return other, other
    head = lax.slice_in_dim(block, 0, 1, axis=dim)
    tail = lax.slice_in_dim(block, block.shape[dim] - 1, block.shape[dim], axis=dim)
    below = lax.ppermute(tail, axis, [(i, (i + 1) % count) for i in range(count)])
    above = lax.ppermute(head, axis, [((i + 1) % count, i) for i in range(count)])
    return below, above


def spread_halo(block):
    for axis, dim in (("dx", 0), ("dy", 1)):
        below, above = neighbours_along(block, axis, dim)
        below = lax.slice_in_dim(below, below.shape[dim] - 1, below.shape[dim], axis=dim)
        above = lax.slice_in_dim(above, 0, 1, axis=dim)
        block = jnp.concatenate([below, block, above], axis=dim)
    return (block,) + neighbours_along(block, "dz", 2)


def pack_kernel(*refs):
    sources, held, fetched = refs[:7], refs[11:18], refs[18]
    atoms_ref, block_ref, own_ref, channel_ref = refs[7:11]
    copies = [
        pltpu.make_async_copy(source, here, fetched.at[at])
        for at, (source, here) in enumerate(zip(sources, held))
    ]
    for copy in copies:
        copy.start()
    for copy in copies:
        copy.wait()
    state_ref, base_ref, frac_ref, charge_ref, live_ref, radial_ref, force_ref = held
    channel_ref[...] = jnp.concatenate([radial_ref[...], force_ref[...]], axis=0)
    slots = state_ref.shape[3]
    sevens = []
    fours = []
    for octant in range(8):
        at = (octant // 4, octant // 2 % 2, slice(octant % 2, octant % 2 + 1))
        charge = charge_ref[at]
        base = jnp.concatenate([base_ref[(d,) + at] for d in range(3)], axis=0).astype(jnp.float32)
        frac = jnp.concatenate([frac_ref[(d,) + at] for d in range(3)], axis=0)
        places = base + frac
        sevens.append(jnp.concatenate([charge, base, frac], axis=0))
        fours.append(jnp.concatenate([places, live_ref[at].astype(jnp.float32)], axis=0))
        pieces = []
        rest = places
        for _ in range(3):
            piece = rest.astype(jnp.bfloat16).astype(jnp.float32)
            pieces.append(piece)
            rest = rest - piece
        pieces.append(jnp.zeros((3, 128 - 3 * slots), jnp.float32))
        cells = jnp.concatenate(pieces, axis=1)
        cells = jnp.concatenate([cells, jnp.zeros((13, 128), jnp.float32)], axis=0)
        block_ref[octant, slots:, :] = cells.astype(jnp.bfloat16)
        block_ref[octant, :slots, :] = state_ref[octant // 4, octant // 2 % 2, octant % 2]
    seven = jnp.concatenate(sevens, axis=1)
    for copy in range(atoms_ref.shape[0]):
        atoms_ref[copy] = seven
    four = jnp.concatenate(fours, axis=1)
    four = jnp.concatenate([four, jnp.zeros_like(four)], axis=0)
    own_ref[...] = jnp.transpose(four)


def pack_atoms(node_state, mesh_base, mesh_frac, charge, nbr_count, radial_weight, force_weight):
    slots, channels = node_state.shape[3:]
    groups = lax.axis_size("dy") * lax.axis_size("dz")
    arrays = (
        node_state,
        mesh_base,
        mesh_frac,
        charge,
        nbr_count,
        radial_weight,
        force_weight[None],
    )
    atoms, block, own_rows, channel_rows = pl.pallas_call(
        pack_kernel,
        out_shape=[
            jax.ShapeDtypeStruct((groups, 7, 8 * slots), jnp.float32),
            jax.ShapeDtypeStruct((8, slots + 16, channels), jnp.bfloat16),
            jax.ShapeDtypeStruct((8 * slots, 8), jnp.float32),
            jax.ShapeDtypeStruct((radial_weight.shape[0] + 1, channels), jnp.float32),
        ],
        in_specs=[pl.BlockSpec(memory_space=pltpu.HBM)] * len(arrays),
        scratch_shapes=[pltpu.VMEM(array.shape, array.dtype) for array in arrays]
        + [pltpu.SemaphoreType.DMA((len(arrays),))],
        compiler_params=pltpu.CompilerParams(vmem_limit_bytes=4 << 20),
    )(*[pltpu.with_memory_space_constraint(array, pltpu.HBM) for array in arrays])
    block = block.reshape(2, 2, 2, slots + 16, channels)
    return atoms, block, own_rows, channel_rows


def count_kernel(code_ref, own_ref, *refs):
    count_ref, chosen_ref = refs[-2:]
    octants, tiles, slots, _ = count_ref.shape
    row_of = lax.broadcasted_iota(jnp.int32, (8, 128), 0)
    lane_of = lax.broadcasted_iota(jnp.int32, (8, 128), 1)
    row_pair = lax.broadcasted_iota(jnp.int32, (16, 128), 0)
    cell_iota = lax.broadcasted_iota(jnp.int32, (128, 128), 0).astype(jnp.float32).astype(jnp.bfloat16)
    one = jnp.ones((128, 128), jnp.bfloat16)
    zero = jnp.zeros((128, 128), jnp.bfloat16)
    lane_float = lane_of.astype(jnp.float32)
    pieces = [(octant, block) for octant in range(octants) for block in range(slots // 8)]
    for octant, block in pieces:
        rows = slice(octant * slots + 8 * block, octant * slots + 8 * block + 8)
        codes = code_ref[rows, :]
        live = lane_float < own_ref[rows, 3:4]
        high = jnp.where(live, codes >> 7, 64)
        low = (codes & 127).astype(jnp.float32)
        for pair in range(0, 8, 2):
            low_hot = []
            high_hot = []
            for atom in (pair, pair + 1):
                low_row = jnp.broadcast_to(low[atom : atom + 1], (16, 128)).astype(jnp.bfloat16)
                low_row = jnp.concatenate([low_row] * 8, axis=0)
                low_hot.append(jnp.where(cell_iota == low_row, one, zero))
                hot = row_pair == high[atom : atom + 1] + 8 * (atom - pair)
                high_hot.append(hot.astype(jnp.float32).astype(jnp.bfloat16))
            counted = lax.dot_general(
                jnp.concatenate(high_hot, axis=1),
                jnp.concatenate(low_hot, axis=1),
                (((1,), (1,)), ((), ())),
                preferred_element_type=jnp.float32,
            )
            count_ref[octant, :, 8 * block + pair, :] = counted[:tiles]
            count_ref[octant, :, 8 * block + pair + 1, :] = counted[8 : 8 + tiles]
    for octant, block in pieces:
        own = slice(8 * block, 8 * block + 8)
        best = jnp.full((8, 128), -1.0, jnp.float32)
        for tile in range(tiles):
            times = count_ref[octant, tile, own, :]
            split = (times == 3.0) | ((times > 4.0) & (times < 8.0))
            best = jnp.where(split, lane_float + 128.0 * tile, best)
        chosen = jnp.max(best, axis=1, keepdims=True)
        rows = slice(octant * slots + 8 * block, octant * slots + 8 * block + 8)
        chosen_ref[rows, :] = jnp.broadcast_to(chosen, (8, 128))
        rest = jnp.zeros((8, 128), jnp.float32)
        for tile in range(tiles):
            times = count_ref[octant, tile, own, :]
            hot = lane_float + 128.0 * tile == chosen
            part = jnp.where(times > 4.0, times - 4.0, times - 2.0)
            rest = rest + jnp.where(hot, part, 0.0)
            count_ref[octant, tile, own, :] = jnp.where(hot, times - part, times)
        total = jnp.sum(rest, axis=1, keepdims=True)
        spare = lane_of - (128 - slots) == row_of + 8 * block
        last = count_ref[octant, tiles - 1, own, :]
        count_ref[octant, tiles - 1, own, :] = jnp.where(spare, total, last)


def neighbour_kernel(
    sizes,
    block_ref,
    below_ref,
    above_ref,
    count_ref,
    chosen_ref,
    own_ref,
    radial_ref,
    mix_ref,
    next_ref,
    push_ref,
    halo_ref,
    place_ref,
    state_ref,
    table_ref,
    message_ref,
    *edge_refs,
):
    count_x, count_y, count_z, slots, basis = sizes
    octant = pl.program_id(0)
    columns = state_ref.shape[1]
    tiles = columns // 128
    per_tile = 128 // slots
    couples = slots // 16
    atoms = 8 * slots
    corner = ((octant // 4) * 4 + octant // 2 % 2) * 4 + octant % 2
    sides = [(side // 9 * 4 + side // 3 % 3) * 4 + side % 3 for side in range(27)]
    row_of = lax.broadcasted_iota(jnp.int32, (8, 128), 0)
    lane_of = lax.broadcasted_iota(jnp.int32, (8, 128), 1)
    lane_float = lane_of.astype(jnp.float32)
    here = octant % 2
    before = 1 - here

    @pl.when(octant == 0)
    def _():
        half = MB // 2
        for parity in range(2):
            state_ref[parity, 27 * slots :, :] = jnp.zeros((slots, 128), jnp.bfloat16)
        starts = [2 * lax.axis_index(axis) - 1 for axis in ("dx", "dy", "dz")]

        def unwrapped(place, start, count):
            reach = start + place
            below = jnp.where(reach < 0, -2 * count * half, 0)
            return jnp.where(reach >= 2 * count, 2 * count * half, below).astype(jnp.float32)

        @pl.loop(0, 16, unroll=2)
        def _(column):
            shift_x = unwrapped(column // 4, starts[0], count_x)
            shift_y = unwrapped(column % 4, starts[1], count_y)
            for level in range(4):
                if level == 0:
                    source = below_ref.at[column, below_ref.shape[1] - 1]
                elif level == 3:
                    source = above_ref.at[column, 0]
                else:
                    source = block_ref.at[column, level - 1]
                cell = column * 4 + level
                halo_ref[cell] = source[:slots, :]
                rows = source[slots:, :].astype(jnp.float32)[:8]
                total = rows + pltpu.roll(rows, 128 - slots, 1)
                total = total + pltpu.roll(rows, 128 - 2 * slots, 1)
                shift_z = unwrapped(level, starts[2], count_z)
                shift = jnp.where(row_of == 0, shift_x, jnp.where(row_of == 1, shift_y, shift_z))
                place_ref[cell] = total + shift

    for tile in range(tiles):
        joined = jnp.zeros((8, 128), jnp.float32)
        for part in range(per_tile):
            side = tile * per_tile + part
            if side < 27:
                moved = place_ref[corner + sides[side]]
                if part:
                    moved = pltpu.roll(moved, part * slots, 1)
                joined = jnp.where(lane_of // slots == part, moved, joined)
        table_ref[tile] = joined

    chosen = chosen_ref[...]
    wide_lane = lax.broadcasted_iota(jnp.int32, (slots, 128), 1).astype(jnp.float32)
    hots = jnp.concatenate(
        [jnp.where(wide_lane + 128.0 * tile == chosen, 1.0, 0.0) for tile in range(tiles)], axis=1
    ).astype(jnp.bfloat16)
    pieces = []
    spots = jnp.concatenate([table_ref[tile] for tile in range(tiles)], axis=1)
    for _ in range(3):
        piece = spots.astype(jnp.bfloat16).astype(jnp.float32)
        pieces.append(piece)
        spots = spots - piece
    pieces = jnp.concatenate(pieces + [jnp.zeros_like(spots)], axis=0).astype(jnp.bfloat16)
    found = lax.dot_general(
        pieces, hots, (((1,), (1,)), ((), ())), preferred_element_type=jnp.float32
    )
    found = (found[:8] + found[8:16]) + found[16:24]
    table_ref[tiles - 1] = jnp.where(
        lane_of < 128 - slots, table_ref[tiles - 1], jnp.concatenate([found] * per_tile, axis=1)
    )

    root_three = math.sqrt(3.0)
    root_fifteen = math.sqrt(15.0)
    root_five = math.sqrt(5.0)
    rates = [
        -(cell_size**2) / (sigma_low * sigma_rate**b) ** 2 * math.log2(math.e) for b in range(basis)
    ]

    def fill_edges(block):
        rows = slice(8 * block, 8 * block + 8)
        edge_ref = edge_refs[block // 2 % 2]
        offset = block % 2 * 9 * basis * 8
        own = own_ref[rows, :]
        for tile in range(tiles):
            times = count_ref[0, tile, rows, :]
            spots = table_ref[tile]
            dx = spots[0:1] - own[:, 0:1]
            dy = spots[1:2] - own[:, 1:2]
            dz = spots[2:3] - own[:, 2:3]
            square = dx * dx + dy * dy + dz * dz
            scale = lax.rsqrt(square + 1.0)
            ux = dx * scale
            uy = dy * scale
            uz = dz * scale
            tx = root_fifteen * ux
            angular = [
                None,
                root_three * ux,
                root_three * uy,
                root_three * uz,
                tx * uy,
                root_fifteen * uy * uz,
                0.5 * root_five * (3.0 * uz * uz - 1.0),
                tx * uz,
                0.5 * root_fifteen * (ux * ux - uy * uy),
            ]
            for pair in range(basis // 2):
                first = times * jnp.exp2(square * rates[2 * pair])
                second = times * jnp.exp2(square * rates[2 * pair + 1])
                for degree in range(9):
                    if degree:
                        parts = [first * angular[degree], second * angular[degree]]
                    else:
                        parts = [first, second]
                    at = offset + (degree * basis + 2 * pair) * 8
                    edge_ref[tile, at : at + 16, :] = jnp.concatenate(parts, axis=0).astype(
                        jnp.bfloat16
                    )

    def add_up(couple, parity, first_row):
        edge_ref = edge_refs[couple % 2]
        edges = jnp.concatenate([edge_ref[tile] for tile in range(tiles)], axis=1)
        summed = jnp.dot(edges, state_ref[parity], preferred_element_type=jnp.float32)
        for half in range(2):
            offset = half * 9 * basis * 8
            for degree in range(9):
                at = offset + degree * basis * 8
                total = summed[at : at + 8] * radial_ref[0:1, :]
                for b in range(1, basis):
                    at = offset + (degree * basis + b) * 8
                    total = total + summed[at : at + 8] * radial_ref[b : b + 1, :]
                message_ref[degree, pl.ds(first_row + 8 * half, 8), :] = total * (
                    1.0 / math.sqrt(NBR)
                )

    def row_start(couple):
        return pl.multiple_of(octant * slots + 16 * couple, 8)

    fill_edges(0)
    fill_edges(1)
    add_up(couples - 1, before, pl.multiple_of((octant * slots + atoms - 16) % atoms, 8))
    for side in range(27):
        state_ref[here, side * slots : (side + 1) * slots, :] = halo_ref[corner + sides[side]]
    state_ref[here, 27 * slots :, :] = jnp.dot(
        hots, state_ref[here], preferred_element_type=jnp.float32
    ).astype(jnp.bfloat16)
    for couple in range(1, couples):
        fill_edges(2 * couple)
        fill_edges(2 * couple + 1)
        add_up(couple - 1, here, row_start(couple - 1))

    @pl.when(octant == 7)
    def _():
        add_up(couples - 1, here, row_start(couples - 1))
        invariant = jnp.dot(
            message_ref[0].astype(jnp.bfloat16), mix_ref[0], preferred_element_type=jnp.float32
        )
        for degree in range(4, 9):
            tensor = jnp.dot(
                message_ref[degree].astype(jnp.bfloat16), mix_ref[2], preferred_element_type=jnp.float32
            )
            invariant = invariant + tensor * tensor
        gating = 1.0 / (1.0 + jnp.exp(-invariant))
        lifted = invariant * gating
        for own in range(8):
            at = ((1 + own // 4) * 4 + 1 + own // 2 % 2) * 4 + 1 + own % 2
            rows = slice(own * slots, (own + 1) * slots)
            next_ref[rows, :] = (halo_ref[at].astype(jnp.float32) + lifted[rows]).astype(jnp.bfloat16)
        weighted = gating * radial_ref[basis : basis + 1, :]
        for k in range(3):
            vector = jnp.dot(
                message_ref[1 + k].astype(jnp.bfloat16), mix_ref[1], preferred_element_type=jnp.float32
            )
            high, low = halves(vector * weighted)
            pushed = lax.dot_general(
                jnp.ones((8, 256), jnp.bfloat16),
                jnp.concatenate([high, low], axis=1).astype(jnp.bfloat16),
                (((1,), (1,)), ((), ())),
                preferred_element_type=jnp.float32,
            )
            push_ref[k : k + 1, :] = pushed[0:1]


def list_counts(nbr_code, own_rows, first, number, earlier):
    slots = nbr_code.shape[3]
    tiles = 28 * slots // 128
    together = 2
    start = first // together
    return pl.pallas_call(
        count_kernel,
        grid=(number // together,),
        in_specs=[
            pl.BlockSpec((together * slots, NBR), lambda o: (o + start, 0)),
            pl.BlockSpec((together * slots, 8), lambda o: (o + start, 0)),
        ]
        + [pl.BlockSpec(memory_space=pl.ANY)] * len(earlier),
        out_specs=[
            pl.BlockSpec((together, tiles, slots, 128), lambda o: (o + start, 0, 0, 0)),
            pl.BlockSpec((together * slots, 128), lambda o: (o + start, 0)),
        ],
        out_shape=[
            jax.ShapeDtypeStruct((8, tiles, slots, 128), jnp.float32),
            jax.ShapeDtypeStruct((8 * slots, 128), jnp.float32),
        ],
        input_output_aliases={2: 0, 3: 1} if earlier else {},
        cost_estimate=pl.CostEstimate(
            flops=1_000_000_000, bytes_accessed=700_000, transcendentals=0
        ),
        compiler_params=pltpu.CompilerParams(vmem_limit_bytes=6 << 20),
    )(nbr_code.reshape(8 * slots, NBR), own_rows, *earlier)


def neighbour_sums(packed, counts, chosen, own_rows, channel_rows, mix_weight):
    tiles, slots = counts.shape[1:3]
    channels = packed[0].shape[-1]
    packed = [block.reshape((16, -1) + block.shape[3:]) for block in packed]
    basis = channel_rows.shape[0] - 1
    columns = 28 * slots
    sizes = (lax.axis_size("dx"), lax.axis_size("dy"), lax.axis_size("dz"), slots, basis)
    edges = pltpu.VMEM((tiles, 9 * basis * 16, 128), jnp.bfloat16)
    whole = lambda *shape: pl.BlockSpec(shape, lambda o: (0,) * len(shape))
    return pl.pallas_call(
        functools.partial(neighbour_kernel, sizes),
        grid=(8,),
        in_specs=[
            *[whole(*block.shape) for block in packed],
            pl.BlockSpec((1, tiles, slots, 128), lambda o: (o, 0, 0, 0)),
            pl.BlockSpec((slots, 128), lambda o: (o, 0)),
            pl.BlockSpec((slots, 8), lambda o: (o, 0)),
            whole(basis + 1, channels),
            whole(3, channels, channels),
        ],
        out_specs=[whole(8 * slots, channels), whole(3, 8 * slots)],
        out_shape=[
            jax.ShapeDtypeStruct((8 * slots, channels), jnp.bfloat16),
            jax.ShapeDtypeStruct((3, 8 * slots), jnp.float32),
        ],
        scratch_shapes=[
            pltpu.VMEM((64, slots, channels), jnp.bfloat16),
            pltpu.VMEM((64, 8, 128), jnp.float32),
            pltpu.VMEM((2, columns, channels), jnp.bfloat16),
            pltpu.VMEM((tiles, 8, 128), jnp.float32),
            pltpu.VMEM((9, 8 * slots, channels), jnp.float32),
            edges,
            edges,
        ],
        compiler_params=pltpu.CompilerParams(vmem_limit_bytes=16 << 20),
        cost_estimate=pl.CostEstimate(
            flops=8_000_000_000, bytes_accessed=2_000_000, transcendentals=2_000_000
        ),
    )(
        *packed,
        counts,
        chosen,
        own_rows,
        channel_rows,
        mix_weight,
    )


def spline_rows(fraction):
    remainder = 1.0 - fraction
    square = fraction * fraction
    cube = square * fraction
    weights = [
        remainder * remainder * remainder / 6.0,
        (3.0 * cube - 6.0 * square + 4.0) / 6.0,
        (-3.0 * cube + 3.0 * square + 3.0 * fraction + 1.0) / 6.0,
        cube / 6.0,
    ]
    slopes = [
        -0.5 * remainder * remainder,
        1.5 * square - 2.0 * fraction,
        -1.5 * square + fraction + 0.5,
        0.5 * square,
    ]
    return weights, slopes


def turn(steps, extent):
    _, width = steps.shape
    parts = -(-extent // 128)
    lane = lax.broadcasted_iota(jnp.int32, (8, 128), 1)
    lines = [
        jnp.cos((lane + 128 * part).astype(jnp.float32) * (2.0 * math.pi / extent))[:1]
        for part in range(parts)
    ]

    def look(index):
        if extent & (extent - 1):
            index = index % extent
        else:
            index = index & (extent - 1)
        found = []
        for start in range(0, width, 128):
            piece = index[:, start : start + 128]
            result = None
            for part in range(parts):
                line = jnp.broadcast_to(lines[part], piece.shape)
                at = piece & 127 if parts > 1 else piece
                here = jnp.take_along_axis(line, at, axis=1)
                result = here if result is None else jnp.where(piece >> 7 == part, here, result)
            found.append(result)
        return jnp.concatenate(found, axis=1) if len(found) > 1 else found[0]

    return look(steps), look(steps + 3 * extent // 4)


def wave_factors(modes, base_row, extent):
    rows = modes.shape[0]
    width = base_row.shape[1]
    wide = jnp.broadcast_to(modes[:, :1], (rows, width))
    first = turn(wide * base_row, extent)
    steps = [turn(modes * t, extent) for t in (1, 2, 3)]
    steps = [tuple(jnp.concatenate([p] * (width // 128), axis=1) for p in pair) for pair in steps]
    return first, steps


def wave_of(factors, coeff):
    (cos_first, sin_first), steps = factors
    part_re = coeff[0] + coeff[1] * steps[0][0] + coeff[2] * steps[1][0] + coeff[3] * steps[2][0]
    part_im = coeff[1] * steps[0][1] + coeff[2] * steps[1][1] + coeff[3] * steps[2][1]
    return cos_first * part_re - sin_first * part_im, sin_first * part_re + cos_first * part_im


def cell_rows(coeff, local_row, cells):
    row_of = lax.broadcasted_iota(jnp.int32, (cells, local_row.shape[1]), 0)
    away = row_of - local_row
    table = jnp.where(away == 3, coeff[3], 0.0)
    for stencil in (2, 1, 0):
        table = jnp.where(away == stencil, coeff[stencil], table)
    return table


def halves(values):
    high = values.astype(jnp.bfloat16).astype(jnp.float32)
    return high, values - high


def wave_start():
    return lax.axis_index("dy") * lax.axis_size("dz") + lax.axis_index("dz")


def spread_kernel(sizes, atoms_ref, sums_ref):
    length_y, length_z, waves, cells = sizes
    groups, _, _ = atoms_ref.shape
    modes_y = wave_start() * waves + lax.broadcasted_iota(jnp.int32, (waves, 128), 0)
    modes_z = 1 + lax.broadcasted_iota(jnp.int32, (KZW, 128), 0)
    anchor = lax.axis_index("dx") * MB
    total = jnp.zeros(sums_ref.shape[1:], jnp.float32)
    for group in range(groups):
        chunk = atoms_ref[group]
        base = chunk[1:4].astype(jnp.int32)
        weights, _ = spline_rows(chunk[4:7])
        row = lambda d: [w[d : d + 1] for w in weights]
        y_re, y_im = wave_of(wave_factors(modes_y, base[1:2], length_y), row(1))
        z_re, z_im = wave_of(wave_factors(modes_z, base[2:3], length_z), row(2))
        mixed_re = []
        mixed_im = []
        for k in range(waves):
            k_re = y_re[k : k + 1]
            k_im = y_im[k : k + 1]
            mixed_re.append(k_re * z_re - k_im * z_im)
            mixed_im.append(-(k_re * z_im + k_im * z_re))
        mixed = jnp.concatenate(mixed_re + mixed_im, axis=0)
        table = cell_rows(row(0), base[0:1] - anchor, cells) * chunk[0:1]
        table_high, table_low = halves(table)
        mixed_high, mixed_low = halves(mixed)
        both = jnp.concatenate([table_high, table_low], axis=0).astype(jnp.bfloat16)
        main = lax.dot_general(
            both,
            mixed_high.astype(jnp.bfloat16),
            (((1,), (1,)), ((), ())),
            preferred_element_type=jnp.float32,
        )
        side = lax.dot_general(
            table_high.astype(jnp.bfloat16),
            mixed_low.astype(jnp.bfloat16),
            (((1,), (1,)), ((), ())),
            preferred_element_type=jnp.float32,
        )
        total = total + (main[:cells] + (main[cells:] + side))
    for copy in range(sums_ref.shape[0]):
        sums_ref[copy] = total


def push_kernel(sizes, atoms_ref, sums_ref, force_ref):
    length_x, length_y, length_z, waves, cells = sizes
    groups, _, width = atoms_ref.shape
    modes = waves * KZW
    start = wave_start() * waves
    modes_y = start + lax.broadcasted_iota(jnp.int32, (waves, 128), 0)
    modes_z = 1 + lax.broadcasted_iota(jnp.int32, (KZW, 128), 0)
    anchor = lax.axis_index("dx") * MB

    count_x = length_x // MB
    lined = -(-count_x * cells // 128) * 128
    place = lax.broadcasted_iota(jnp.int32, (1, lined), 1)
    place = place + (MB - cells) * (place // cells)
    mode = lax.broadcasted_iota(jnp.int32, (length_x, lined), 0)
    forward = jnp.concatenate(turn(mode * place, length_x), axis=0)[:, : count_x * cells]
    turned = jnp.dot(
        forward, sums_ref[...], precision=highest, preferred_element_type=jnp.float32
    )
    cosine = turned[:length_x]
    sine = turned[length_x:]

    def folded(number, extent):
        number = jnp.where(2 * number >= extent, number - extent, number)
        return number.astype(jnp.float32) / (cell_size * extent)

    mode_shape = (length_x, modes)
    mode_x = lax.broadcasted_iota(jnp.int32, mode_shape, 0)
    mode_lane = lax.broadcasted_iota(jnp.int32, mode_shape, 1)
    wave_square = (
        jnp.square(folded(mode_x, length_x))
        + jnp.square(folded(start + mode_lane // KZW, length_y))
        + jnp.square(folded(mode_lane % KZW + 1, length_z))
    )
    volume = cell_size**3 * length_x * length_y * length_z
    green = (
        coulomb
        / (math.pi * volume)
        * jnp.exp(-(math.pi**2) * wave_square / ewald_beta**2)
        / wave_square
    )
    scaled = jnp.concatenate(
        [
            green * (cosine[:, :modes] + sine[:, modes:]),
            green * (cosine[:, modes:] - sine[:, :modes]),
        ],
        axis=1,
    )
    cell = anchor + lax.broadcasted_iota(jnp.int32, (cells, length_x), 0)
    mode = lax.broadcasted_iota(jnp.int32, (cells, length_x), 1)
    lines = jnp.concatenate(turn(cell * mode, length_x), axis=0)
    turned = jnp.dot(lines, scaled, precision=highest, preferred_element_type=jnp.float32)
    cosine = turned[:cells]
    sine = turned[cells:]
    back = jnp.concatenate(
        [cosine[:, :modes] - sine[:, modes:], sine[:, :modes] + cosine[:, modes:]], axis=1
    )
    back_high, back_low = halves(back)
    spare = jnp.zeros((128 - 3 * cells, 2 * modes), jnp.float32)
    stacked = jnp.concatenate([back_high, back_high, back_low, spare], axis=0)
    stacked = jnp.transpose(stacked).astype(jnp.bfloat16)

    for group in range(groups):
        chunk = atoms_ref[group]
        base = chunk[1:4].astype(jnp.int32)
        weights, slopes = spline_rows(chunk[4:7])
        row = lambda d: [w[d : d + 1] for w in weights]
        tilt = lambda d: [w[d : d + 1] for w in slopes]
        factors_y = wave_factors(modes_y, base[1:2], length_y)
        factors_z = wave_factors(modes_z, base[2:3], length_z)
        y_re, y_im = wave_of(factors_y, row(1))
        dy_re, dy_im = wave_of(factors_y, tilt(1))
        z_re, z_im = wave_of(factors_z, row(2))
        dz_re, dz_im = wave_of(factors_z, tilt(2))

        def on_atoms(coeff):
            high, low = halves(cell_rows(coeff, base[0:1] - anchor, cells))
            none = jnp.zeros((128 - 3 * cells, width), jnp.float32)
            right = jnp.concatenate([high, low, high, none], axis=0).astype(jnp.bfloat16)
            return jnp.dot(stacked, right, preferred_element_type=jnp.float32)

        value = on_atoms(row(0))
        slant = on_atoms(tilt(0))

        def along(field, wave_re, wave_im):
            sum_re = jnp.zeros((KZW, width), jnp.float32)
            sum_im = jnp.zeros((KZW, width), jnp.float32)
            for k in range(waves):
                f_re = field[k * KZW : (k + 1) * KZW]
                f_im = field[modes + k * KZW : modes + (k + 1) * KZW]
                k_re = wave_re[k : k + 1]
                k_im = wave_im[k : k + 1]
                sum_re = sum_re + (f_re * k_re - f_im * k_im)
                sum_im = sum_im + (f_re * k_im + f_im * k_re)
            return sum_re, sum_im

        def ended(pair, wave_re, wave_im):
            return 2.0 * jnp.sum(pair[0] * wave_re - pair[1] * wave_im, axis=0, keepdims=True)

        push_x = ended(along(slant, y_re, y_im), z_re, z_im)
        push_y = ended(along(value, dy_re, dy_im), z_re, z_im)
        push_z = ended(along(value, y_re, y_im), dz_re, dz_im)
        force_ref[group] = jnp.concatenate([push_x, push_y, push_z], axis=0) * (
            -chunk[0:1] / cell_size
        )


def long_range(packed, counts):
    count_x = lax.axis_size("dx")
    count_y = lax.axis_size("dy")
    count_z = lax.axis_size("dz")
    groups, _, atom_total = packed.shape
    cells = -(-(MB + 3) // 8) * 8
    length_x = MB * count_x
    length_y = MB * count_y
    length_z = MB * count_z
    waves = MB // count_z
    modes = waves * KZW
    atoms = lax.all_to_all(packed, ("dy", "dz"), 0, 0, tiled=True)
    sums = pl.pallas_call(
        functools.partial(spread_kernel, (length_y, length_z, waves, cells)),
        out_shape=jax.ShapeDtypeStruct((count_x, cells, 2 * modes), jnp.float32),
        compiler_params=pltpu.CompilerParams(vmem_limit_bytes=8 << 20),
    )(atoms)
    received = lax.all_to_all(sums, "dx", 0, 0, tiled=True)
    received = received.reshape(count_x * cells, 2 * modes)
    received, counts = lax.optimization_barrier((received, counts))
    parts = pl.pallas_call(
        functools.partial(push_kernel, (length_x, length_y, length_z, waves, cells)),
        out_shape=jax.ShapeDtypeStruct((groups, 3, atom_total), jnp.float32),
        compiler_params=pltpu.CompilerParams(vmem_limit_bytes=16 << 20),
    )(atoms, received)
    parts = lax.all_to_all(parts, ("dy", "dz"), 0, 0, tiled=True)
    return jnp.sum(parts, axis=0), counts


def shards(
    node_state,
    mesh_base,
    mesh_frac,
    charge,
    nbr_code,
    nbr_count,
    radial_weight,
    mix_weight,
    force_weight,
):
    octants = node_state.shape[3]
    packed, block, own_rows, channel_rows = pack_atoms(
        node_state, mesh_base, mesh_frac, charge, nbr_count, radial_weight, force_weight
    )
    earlier = list_counts(nbr_code, own_rows, 0, 2, ())
    counts, chosen = list_counts(nbr_code, own_rows, 2, 6, earlier)
    long_force, counts = long_range(packed, counts)
    packed_halo = spread_halo(block)
    updated, short_force = neighbour_sums(
        packed_halo, counts, chosen, own_rows, channel_rows, mix_weight
    )
    node_next = updated.reshape(node_state.shape)
    forces = (short_force + long_force).reshape(3, 2, 2, 2, octants)
    return (node_next, forces)


def solution(mesh):
    placed = (
        P("dx", "dy", "dz", None, None),
        P(None, "dx", "dy", "dz", None),
        P(None, "dx", "dy", "dz", None),
        P("dx", "dy", "dz", None),
        P("dx", "dy", "dz", None, None),
        P("dx", "dy", "dz", None),
        P(),
        P(),
        P(),
    )

    return jax.shard_map(
        shards,
        mesh=mesh,
        in_specs=placed,
        out_specs=(P("dx", "dy", "dz", None, None), P(None, "dx", "dy", "dz", None)),
        check_vma=False,
    )
```

```python
import functools
import math

import jax
import jax.numpy as jnp
from jax import lax
from jax.experimental import pallas as pl
from jax.experimental.pallas import tpu as pltpu
from jax.sharding import PartitionSpec as P


NBR = 128
MB = 32
KZW = 8


cell_size = 1.13
ewald_beta = 0.625
coulomb = 332.0637
sigma_low = 8.0
sigma_rate = 1.5


def neighbours_along(block, axis, dim):
    count = lax.axis_size(axis)
    if count == 2:
        other = lax.ppermute(block, axis, [(0, 1), (1, 0)])
        return other, other
    head = lax.slice_in_dim(block, 0, 1, axis=dim)
    tail = lax.slice_in_dim(block, block.shape[dim] - 1, block.shape[dim], axis=dim)
    below = lax.ppermute(tail, axis, [(i, (i + 1) % count) for i in range(count)])
    above = lax.ppermute(head, axis, [((i + 1) % count, i) for i in range(count)])
    return below, above


def spread_halo(block):
    for axis, dim in (("dx", 0), ("dy", 1)):
        below, above = neighbours_along(block, axis, dim)
        below = lax.slice_in_dim(below, below.shape[dim] - 1, below.shape[dim], axis=dim)
        above = lax.slice_in_dim(above, 0, 1, axis=dim)
        block = jnp.concatenate([below, block, above], axis=dim)
    return (block,) + neighbours_along(block, "dz", 2)


def pack_kernel(*refs):
    sources, held, fetched = refs[:7], refs[11:18], refs[18]
    atoms_ref, block_ref, own_ref, channel_ref = refs[7:11]
    copies = [
        pltpu.make_async_copy(source, here, fetched.at[at])
        for at, (source, here) in enumerate(zip(sources, held))
    ]
    for copy in copies:
        copy.start()
    for copy in copies:
        copy.wait()
    state_ref, base_ref, frac_ref, charge_ref, live_ref, radial_ref, force_ref = held
    channel_ref[...] = jnp.concatenate([radial_ref[...], force_ref[...]], axis=0)
    slots = state_ref.shape[3]
    sevens = []
    fours = []
    for octant in range(8):
        at = (octant // 4, octant // 2 % 2, slice(octant % 2, octant % 2 + 1))
        charge = charge_ref[at]
        base = jnp.concatenate([base_ref[(d,) + at] for d in range(3)], axis=0).astype(jnp.float32)
        frac = jnp.concatenate([frac_ref[(d,) + at] for d in range(3)], axis=0)
        places = base + frac
        sevens.append(jnp.concatenate([charge, base, frac], axis=0))
        fours.append(jnp.concatenate([places, live_ref[at].astype(jnp.float32)], axis=0))
        pieces = []
        rest = places
        for _ in range(3):
            piece = rest.astype(jnp.bfloat16).astype(jnp.float32)
            pieces.append(piece)
            rest = rest - piece
        pieces.append(jnp.zeros((3, 128 - 3 * slots), jnp.float32))
        cells = jnp.concatenate(pieces, axis=1)
        cells = jnp.concatenate([cells, jnp.zeros((13, 128), jnp.float32)], axis=0)
        block_ref[octant, slots:, :] = cells.astype(jnp.bfloat16)
        block_ref[octant, :slots, :] = state_ref[octant // 4, octant // 2 % 2, octant % 2]
    seven = jnp.concatenate(sevens, axis=1)
    for copy in range(atoms_ref.shape[0]):
        atoms_ref[copy] = seven
    four = jnp.concatenate(fours, axis=1)
    four = jnp.concatenate([four, jnp.zeros_like(four)], axis=0)
    own_ref[...] = jnp.transpose(four)


def pack_atoms(node_state, mesh_base, mesh_frac, charge, nbr_count, radial_weight, force_weight):
    slots, channels = node_state.shape[3:]
    groups = lax.axis_size("dy") * lax.axis_size("dz")
    arrays = (
        node_state,
        mesh_base,
        mesh_frac,
        charge,
        nbr_count,
        radial_weight,
        force_weight[None],
    )
    atoms, block, own_rows, channel_rows = pl.pallas_call(
        pack_kernel,
        out_shape=[
            jax.ShapeDtypeStruct((groups, 7, 8 * slots), jnp.float32),
            jax.ShapeDtypeStruct((8, slots + 16, channels), jnp.bfloat16),
            jax.ShapeDtypeStruct((8 * slots, 8), jnp.float32),
            jax.ShapeDtypeStruct((radial_weight.shape[0] + 1, channels), jnp.float32),
        ],
        in_specs=[pl.BlockSpec(memory_space=pltpu.HBM)] * len(arrays),
        scratch_shapes=[pltpu.VMEM(array.shape, array.dtype) for array in arrays]
        + [pltpu.SemaphoreType.DMA((len(arrays),))],
        compiler_params=pltpu.CompilerParams(vmem_limit_bytes=4 << 20),
    )(*[pltpu.with_memory_space_constraint(array, pltpu.HBM) for array in arrays])
    block = block.reshape(2, 2, 2, slots + 16, channels)
    return atoms, block, own_rows, channel_rows


def count_kernel(code_ref, own_ref, *refs):
    count_ref, chosen_ref = refs[-2:]
    octants, tiles, slots, _ = count_ref.shape
    row_of = lax.broadcasted_iota(jnp.int32, (8, 128), 0)
    lane_of = lax.broadcasted_iota(jnp.int32, (8, 128), 1)
    row_pair = lax.broadcasted_iota(jnp.int32, (16, 128), 0)
    cell_iota = lax.broadcasted_iota(jnp.int32, (128, 128), 0).astype(jnp.float32).astype(jnp.bfloat16)
    one = jnp.ones((128, 128), jnp.bfloat16)
    zero = jnp.zeros((128, 128), jnp.bfloat16)
    lane_float = lane_of.astype(jnp.float32)
    pieces = [(octant, block) for octant in range(octants) for block in range(slots // 8)]
    for octant, block in pieces:
        rows = slice(octant * slots + 8 * block, octant * slots + 8 * block + 8)
        codes = code_ref[rows, :]
        live = lane_float < own_ref[rows, 3:4]
        high = jnp.where(live, codes >> 7, 64)
        low = (codes & 127).astype(jnp.float32)
        for pair in range(0, 8, 2):
            low_hot = []
            high_hot = []
            for atom in (pair, pair + 1):
                low_row = jnp.broadcast_to(low[atom : atom + 1], (16, 128)).astype(jnp.bfloat16)
                low_row = jnp.concatenate([low_row] * 8, axis=0)
                low_hot.append(jnp.where(cell_iota == low_row, one, zero))
                hot = row_pair == high[atom : atom + 1] + 8 * (atom - pair)
                high_hot.append(hot.astype(jnp.float32).astype(jnp.bfloat16))
            counted = lax.dot_general(
                jnp.concatenate(high_hot, axis=1),
                jnp.concatenate(low_hot, axis=1),
                (((1,), (1,)), ((), ())),
                preferred_element_type=jnp.float32,
            )
            count_ref[octant, :, 8 * block + pair, :] = counted[:tiles]
            count_ref[octant, :, 8 * block + pair + 1, :] = counted[8 : 8 + tiles]
    for octant, block in pieces:
        own = slice(8 * block, 8 * block + 8)
        best = jnp.full((8, 128), -1.0, jnp.float32)
        for tile in range(tiles):
            times = count_ref[octant, tile, own, :]
            split = (times == 3.0) | ((times > 4.0) & (times < 8.0))
            best = jnp.where(split, lane_float + 128.0 * tile, best)
        chosen = jnp.max(best, axis=1, keepdims=True)
        rows = slice(octant * slots + 8 * block, octant * slots + 8 * block + 8)
        chosen_ref[rows, :] = jnp.broadcast_to(chosen, (8, 128))
        rest = jnp.zeros((8, 128), jnp.float32)
        for tile in range(tiles):
            times = count_ref[octant, tile, own, :]
            hot = lane_float + 128.0 * tile == chosen
            part = jnp.where(times > 4.0, times - 4.0, times - 2.0)
            rest = rest + jnp.where(hot, part, 0.0)
            count_ref[octant, tile, own, :] = jnp.where(hot, times - part, times)
        total = jnp.sum(rest, axis=1, keepdims=True)
        spare = lane_of - (128 - slots) == row_of + 8 * block
        last = count_ref[octant, tiles - 1, own, :]
        count_ref[octant, tiles - 1, own, :] = jnp.where(spare, total, last)


def neighbour_kernel(
    sizes,
    block_ref,
    below_ref,
    above_ref,
    count_ref,
    chosen_ref,
    own_ref,
    radial_ref,
    mix_ref,
    next_ref,
    push_ref,
    halo_ref,
    place_ref,
    state_ref,
    table_ref,
    message_ref,
    *edge_refs,
):
    count_x, count_y, count_z, slots, basis = sizes
    octant = pl.program_id(0)
    columns = state_ref.shape[1]
    tiles = columns // 128
    per_tile = 128 // slots
    couples = slots // 16
    atoms = 8 * slots
    corner = ((octant // 4) * 4 + octant // 2 % 2) * 4 + octant % 2
    sides = [(side // 9 * 4 + side // 3 % 3) * 4 + side % 3 for side in range(27)]
    row_of = lax.broadcasted_iota(jnp.int32, (8, 128), 0)
    lane_of = lax.broadcasted_iota(jnp.int32, (8, 128), 1)
    lane_float = lane_of.astype(jnp.float32)
    here = octant % 2
    before = 1 - here

    @pl.when(octant == 0)
    def _():
        half = MB // 2
        for parity in range(2):
            state_ref[parity, 27 * slots :, :] = jnp.zeros((slots, 128), jnp.bfloat16)
        starts = [2 * lax.axis_index(axis) - 1 for axis in ("dx", "dy", "dz")]

        def unwrapped(place, start, count):
            reach = start + place
            below = jnp.where(reach < 0, -2 * count * half, 0)
            return jnp.where(reach >= 2 * count, 2 * count * half, below).astype(jnp.float32)

        @pl.loop(0, 16, unroll=2)
        def _(column):
            shift_x = unwrapped(column // 4, starts[0], count_x)
            shift_y = unwrapped(column % 4, starts[1], count_y)
            for level in range(4):
                if level == 0:
                    source = below_ref.at[column, below_ref.shape[1] - 1]
                elif level == 3:
                    source = above_ref.at[column, 0]
                else:
                    source = block_ref.at[column, level - 1]
                cell = column * 4 + level
                halo_ref[cell] = source[:slots, :]
                rows = source[slots:, :].astype(jnp.float32)[:8]
                total = rows + pltpu.roll(rows, 128 - slots, 1)
                total = total + pltpu.roll(rows, 128 - 2 * slots, 1)
                shift_z = unwrapped(level, starts[2], count_z)
                shift = jnp.where(row_of == 0, shift_x, jnp.where(row_of == 1, shift_y, shift_z))
                place_ref[cell] = total + shift

    for tile in range(tiles):
        joined = jnp.zeros((8, 128), jnp.float32)
        for part in range(per_tile):
            side = tile * per_tile + part
            if side < 27:
                moved = place_ref[corner + sides[side]]
                if part:
                    moved = pltpu.roll(moved, part * slots, 1)
                joined = jnp.where(lane_of // slots == part, moved, joined)
        table_ref[tile] = joined

    chosen = chosen_ref[...]
    wide_lane = lax.broadcasted_iota(jnp.int32, (slots, 128), 1).astype(jnp.float32)
    hots = jnp.concatenate(
        [jnp.where(wide_lane + 128.0 * tile == chosen, 1.0, 0.0) for tile in range(tiles)], axis=1
    ).astype(jnp.bfloat16)
    pieces = []
    spots = jnp.concatenate([table_ref[tile] for tile in range(tiles)], axis=1)
    for _ in range(3):
        piece = spots.astype(jnp.bfloat16).astype(jnp.float32)
        pieces.append(piece)
        spots = spots - piece
    pieces = jnp.concatenate(pieces + [jnp.zeros_like(spots)], axis=0).astype(jnp.bfloat16)
    found = lax.dot_general(
        pieces, hots, (((1,), (1,)), ((), ())), preferred_element_type=jnp.float32
    )
    found = (found[:8] + found[8:16]) + found[16:24]
    table_ref[tiles - 1] = jnp.where(
        lane_of < 128 - slots, table_ref[tiles - 1], jnp.concatenate([found] * per_tile, axis=1)
    )

    root_three = math.sqrt(3.0)
    root_fifteen = math.sqrt(15.0)
    root_five = math.sqrt(5.0)
    rates = [
        -(cell_size**2) / (sigma_low * sigma_rate**b) ** 2 * math.log2(math.e) for b in range(basis)
    ]

    def fill_edges(block):
        rows = slice(8 * block, 8 * block + 8)
        edge_ref = edge_refs[block // 2 % 2]
        offset = block % 2 * 9 * basis * 8
        own = own_ref[rows, :]
        for tile in range(tiles):
            times = count_ref[0, tile, rows, :]
            spots = table_ref[tile]
            dx = spots[0:1] - own[:, 0:1]
            dy = spots[1:2] - own[:, 1:2]
            dz = spots[2:3] - own[:, 2:3]
            square = dx * dx + dy * dy + dz * dz
            scale = lax.rsqrt(square + 1.0)
            ux = dx * scale
            uy = dy * scale
            uz = dz * scale
            tx = root_fifteen * ux
            angular = [
                None,
                root_three * ux,
                root_three * uy,
                root_three * uz,
                tx * uy,
                root_fifteen * uy * uz,
                0.5 * root_five * (3.0 * uz * uz - 1.0),
                tx * uz,
                0.5 * root_fifteen * (ux * ux - uy * uy),
            ]
            for pair in range(basis // 2):
                first = times * jnp.exp2(square * rates[2 * pair])
                second = times * jnp.exp2(square * rates[2 * pair + 1])
                for degree in range(9):
                    if degree:
                        parts = [first * angular[degree], second * angular[degree]]
                    else:
                        parts = [first, second]
                    at = offset + (degree * basis + 2 * pair) * 8
                    edge_ref[tile, at : at + 16, :] = jnp.concatenate(parts, axis=0).astype(
                        jnp.bfloat16
                    )

    def add_up(couple, parity, first_row):
        edge_ref = edge_refs[couple % 2]
        edges = jnp.concatenate([edge_ref[tile] for tile in range(tiles)], axis=1)
        summed = jnp.dot(edges, state_ref[parity], preferred_element_type=jnp.float32)
        for half in range(2):
            offset = half * 9 * basis * 8
            for degree in range(9):
                at = offset + degree * basis * 8
                total = summed[at : at + 8] * radial_ref[0:1, :]
                for b in range(1, basis):
                    at = offset + (degree * basis + b) * 8
                    total = total + summed[at : at + 8] * radial_ref[b : b + 1, :]
                message_ref[degree, pl.ds(first_row + 8 * half, 8), :] = total * (
                    1.0 / math.sqrt(NBR)
                )

    def row_start(couple):
        return pl.multiple_of(octant * slots + 16 * couple, 8)

    fill_edges(0)
    fill_edges(1)
    add_up(couples - 1, before, pl.multiple_of((octant * slots + atoms - 16) % atoms, 8))
    for side in range(27):
        state_ref[here, side * slots : (side + 1) * slots, :] = halo_ref[corner + sides[side]]
    state_ref[here, 27 * slots :, :] = jnp.dot(
        hots, state_ref[here], preferred_element_type=jnp.float32
    ).astype(jnp.bfloat16)
    for couple in range(1, couples):
        fill_edges(2 * couple)
        fill_edges(2 * couple + 1)
        add_up(couple - 1, here, row_start(couple - 1))

    @pl.when(octant == 7)
    def _():
        add_up(couples - 1, here, row_start(couples - 1))
        invariant = jnp.dot(
            message_ref[0].astype(jnp.bfloat16), mix_ref[0], preferred_element_type=jnp.float32
        )
        for degree in range(4, 9):
            tensor = jnp.dot(
                message_ref[degree].astype(jnp.bfloat16), mix_ref[2], preferred_element_type=jnp.float32
            )
            invariant = invariant + tensor * tensor
        gating = 1.0 / (1.0 + jnp.exp(-invariant))
        lifted = invariant * gating
        for own in range(8):
            at = ((1 + own // 4) * 4 + 1 + own // 2 % 2) * 4 + 1 + own % 2
            rows = slice(own * slots, (own + 1) * slots)
            next_ref[rows, :] = (halo_ref[at].astype(jnp.float32) + lifted[rows]).astype(jnp.bfloat16)
        weighted = gating * radial_ref[basis : basis + 1, :]
        for k in range(3):
            vector = jnp.dot(
                message_ref[1 + k].astype(jnp.bfloat16), mix_ref[1], preferred_element_type=jnp.float32
            )
            high, low = halves(vector * weighted)
            pushed = lax.dot_general(
                jnp.ones((8, 256), jnp.bfloat16),
                jnp.concatenate([high, low], axis=1).astype(jnp.bfloat16),
                (((1,), (1,)), ((), ())),
                preferred_element_type=jnp.float32,
            )
            push_ref[k : k + 1, :] = pushed[0:1]


def list_counts(nbr_code, own_rows, first, number, earlier):
    slots = nbr_code.shape[3]
    tiles = 28 * slots // 128
    together = 2
    start = first // together
    return pl.pallas_call(
        count_kernel,
        grid=(number // together,),
        in_specs=[
            pl.BlockSpec((together * slots, NBR), lambda o: (o + start, 0)),
            pl.BlockSpec((together * slots, 8), lambda o: (o + start, 0)),
        ]
        + [pl.BlockSpec(memory_space=pl.ANY)] * len(earlier),
        out_specs=[
            pl.BlockSpec((together, tiles, slots, 128), lambda o: (o + start, 0, 0, 0)),
            pl.BlockSpec((together * slots, 128), lambda o: (o + start, 0)),
        ],
        out_shape=[
            jax.ShapeDtypeStruct((8, tiles, slots, 128), jnp.float32),
            jax.ShapeDtypeStruct((8 * slots, 128), jnp.float32),
        ],
        input_output_aliases={2: 0, 3: 1} if earlier else {},
        cost_estimate=pl.CostEstimate(
            flops=1_000_000_000, bytes_accessed=700_000, transcendentals=0
        ),
        compiler_params=pltpu.CompilerParams(vmem_limit_bytes=6 << 20),
    )(nbr_code.reshape(8 * slots, NBR), own_rows, *earlier)


def neighbour_sums(packed, counts, chosen, own_rows, channel_rows, mix_weight):
    tiles, slots = counts.shape[1:3]
    channels = packed[0].shape[-1]
    packed = [block.reshape((16, -1) + block.shape[3:]) for block in packed]
    basis = channel_rows.shape[0] - 1
    columns = 28 * slots
    sizes = (lax.axis_size("dx"), lax.axis_size("dy"), lax.axis_size("dz"), slots, basis)
    edges = pltpu.VMEM((tiles, 9 * basis * 16, 128), jnp.bfloat16)
    whole = lambda *shape: pl.BlockSpec(shape, lambda o: (0,) * len(shape))
    return pl.pallas_call(
        functools.partial(neighbour_kernel, sizes),
        grid=(8,),
        in_specs=[
            *[whole(*block.shape) for block in packed],
            pl.BlockSpec((1, tiles, slots, 128), lambda o: (o, 0, 0, 0)),
            pl.BlockSpec((slots, 128), lambda o: (o, 0)),
            pl.BlockSpec((slots, 8), lambda o: (o, 0)),
            whole(basis + 1, channels),
            whole(3, channels, channels),
        ],
        out_specs=[whole(8 * slots, channels), whole(3, 8 * slots)],
        out_shape=[
            jax.ShapeDtypeStruct((8 * slots, channels), jnp.bfloat16),
            jax.ShapeDtypeStruct((3, 8 * slots), jnp.float32),
        ],
        scratch_shapes=[
            pltpu.VMEM((64, slots, channels), jnp.bfloat16),
            pltpu.VMEM((64, 8, 128), jnp.float32),
            pltpu.VMEM((2, columns, channels), jnp.bfloat16),
            pltpu.VMEM((tiles, 8, 128), jnp.float32),
            pltpu.VMEM((9, 8 * slots, channels), jnp.float32),
            edges,
            edges,
        ],
        compiler_params=pltpu.CompilerParams(vmem_limit_bytes=16 << 20),
        cost_estimate=pl.CostEstimate(
            flops=8_000_000_000, bytes_accessed=2_000_000, transcendentals=2_000_000
        ),
    )(
        *packed,
        counts,
        chosen,
        own_rows,
        channel_rows,
        mix_weight,
    )


def spline_rows(fraction):
    remainder = 1.0 - fraction
    square = fraction * fraction
    cube = square * fraction
    weights = [
        remainder * remainder * remainder / 6.0,
        (3.0 * cube - 6.0 * square + 4.0) / 6.0,
        (-3.0 * cube + 3.0 * square + 3.0 * fraction + 1.0) / 6.0,
        cube / 6.0,
    ]
    slopes = [
        -0.5 * remainder * remainder,
        1.5 * square - 2.0 * fraction,
        -1.5 * square + fraction + 0.5,
        0.5 * square,
    ]
    return weights, slopes


def turn(steps, extent):
    _, width = steps.shape
    parts = -(-extent // 128)
    lane = lax.broadcasted_iota(jnp.int32, (8, 128), 1)
    lines = [
        jnp.cos((lane + 128 * part).astype(jnp.float32) * (2.0 * math.pi / extent))[:1]
        for part in range(parts)
    ]

    def look(index):
        if extent & (extent - 1):
            index = index % extent
        else:
            index = index & (extent - 1)
        found = []
        for start in range(0, width, 128):
            piece = index[:, start : start + 128]
            result = None
            for part in range(parts):
                line = jnp.broadcast_to(lines[part], piece.shape)
                at = piece & 127 if parts > 1 else piece
                here = jnp.take_along_axis(line, at, axis=1)
                result = here if result is None else jnp.where(piece >> 7 == part, here, result)
            found.append(result)
        return jnp.concatenate(found, axis=1) if len(found) > 1 else found[0]

    return look(steps), look(steps + 3 * extent // 4)


def wave_factors(modes, base_row, extent):
    rows = modes.shape[0]
    width = base_row.shape[1]
    wide = jnp.broadcast_to(modes[:, :1], (rows, width))
    first = turn(wide * base_row, extent)
    steps = [turn(modes * t, extent) for t in (1, 2, 3)]
    steps = [tuple(jnp.concatenate([p] * (width // 128), axis=1) for p in pair) for pair in steps]
    return first, steps


def wave_of(factors, coeff):
    (cos_first, sin_first), steps = factors
    part_re = coeff[0] + coeff[1] * steps[0][0] + coeff[2] * steps[1][0] + coeff[3] * steps[2][0]
    part_im = coeff[1] * steps[0][1] + coeff[2] * steps[1][1] + coeff[3] * steps[2][1]
    return cos_first * part_re - sin_first * part_im, sin_first * part_re + cos_first * part_im


def cell_rows(coeff, local_row, cells):
    row_of = lax.broadcasted_iota(jnp.int32, (cells, local_row.shape[1]), 0)
    away = row_of - local_row
    table = jnp.where(away == 3, coeff[3], 0.0)
    for stencil in (2, 1, 0):
        table = jnp.where(away == stencil, coeff[stencil], table)
    return table


def halves(values):
    high = values.astype(jnp.bfloat16).astype(jnp.float32)
    return high, values - high


def split_dot(left, right):
    rows = left.shape[0]
    left_high, left_low = halves(left)
    right_high, right_low = halves(right)
    both = jnp.concatenate([left_high, left_low], axis=0).astype(jnp.bfloat16)
    main = jnp.dot(both, right_high.astype(jnp.bfloat16), preferred_element_type=jnp.float32)
    side = jnp.dot(
        left_high.astype(jnp.bfloat16),
        right_low.astype(jnp.bfloat16),
        preferred_element_type=jnp.float32,
    )
    return main[:rows] + (main[rows:] + side)


def wave_start():
    return lax.axis_index("dy") * lax.axis_size("dz") + lax.axis_index("dz")


def spread_kernel(sizes, atoms_ref, sums_ref):
    length_y, length_z, waves, cells = sizes
    groups, _, _ = atoms_ref.shape
    modes_y = wave_start() * waves + lax.broadcasted_iota(jnp.int32, (waves, 128), 0)
    modes_z = 1 + lax.broadcasted_iota(jnp.int32, (KZW, 128), 0)
    anchor = lax.axis_index("dx") * MB
    total = jnp.zeros(sums_ref.shape[1:], jnp.float32)
    for group in range(groups):
        chunk = atoms_ref[group]
        base = chunk[1:4].astype(jnp.int32)
        weights, _ = spline_rows(chunk[4:7])
        row = lambda d: [w[d : d + 1] for w in weights]
        y_re, y_im = wave_of(wave_factors(modes_y, base[1:2], length_y), row(1))
        z_re, z_im = wave_of(wave_factors(modes_z, base[2:3], length_z), row(2))
        mixed_re = []
        mixed_im = []
        for k in range(waves):
            k_re = y_re[k : k + 1]
            k_im = y_im[k : k + 1]
            mixed_re.append(k_re * z_re - k_im * z_im)
            mixed_im.append(-(k_re * z_im + k_im * z_re))
        mixed = jnp.concatenate(mixed_re + mixed_im, axis=0)
        table = cell_rows(row(0), base[0:1] - anchor, cells) * chunk[0:1]
        table_high, table_low = halves(table)
        mixed_high, mixed_low = halves(mixed)
        both = jnp.concatenate([table_high, table_low], axis=0).astype(jnp.bfloat16)
        main = lax.dot_general(
            both,
            mixed_high.astype(jnp.bfloat16),
            (((1,), (1,)), ((), ())),
            preferred_element_type=jnp.float32,
        )
        side = lax.dot_general(
            table_high.astype(jnp.bfloat16),
            mixed_low.astype(jnp.bfloat16),
            (((1,), (1,)), ((), ())),
            preferred_element_type=jnp.float32,
        )
        total = total + (main[:cells] + (main[cells:] + side))
    for copy in range(sums_ref.shape[0]):
        sums_ref[copy] = total


def mesh_tables_kernel(sizes, forward_ref, lines_ref, green_ref):
    length_x, length_y, length_z, waves, cells = sizes
    modes = waves * KZW
    start = wave_start() * waves
    anchor = lax.axis_index("dx") * MB
    count_x = length_x // MB
    lined = -(-count_x * cells // 128) * 128
    place = lax.broadcasted_iota(jnp.int32, (1, lined), 1)
    place = place + (MB - cells) * (place // cells)
    mode = lax.broadcasted_iota(jnp.int32, (length_x, lined), 0)
    forward = jnp.concatenate(turn(mode * place, length_x), axis=0)[:, : count_x * cells]
    forward_ref[...] = forward

    def folded(number, extent):
        number = jnp.where(2 * number >= extent, number - extent, number)
        return number.astype(jnp.float32) / (cell_size * extent)

    mode_shape = (length_x, modes)
    mode_x = lax.broadcasted_iota(jnp.int32, mode_shape, 0)
    mode_lane = lax.broadcasted_iota(jnp.int32, mode_shape, 1)
    wave_square = (
        jnp.square(folded(mode_x, length_x))
        + jnp.square(folded(start + mode_lane // KZW, length_y))
        + jnp.square(folded(mode_lane % KZW + 1, length_z))
    )
    volume = cell_size**3 * length_x * length_y * length_z
    green = (
        coulomb
        / (math.pi * volume)
        * jnp.exp(-(math.pi**2) * wave_square / ewald_beta**2)
        / wave_square
    )
    green_ref[...] = green
    cell = anchor + lax.broadcasted_iota(jnp.int32, (cells, length_x), 0)
    mode = lax.broadcasted_iota(jnp.int32, (cells, length_x), 1)
    lines = jnp.concatenate(turn(cell * mode, length_x), axis=0)
    lines_ref[...] = lines


def push_kernel(sizes, atoms_ref, sums_ref, forward_ref, lines_ref, green_ref, force_ref):
    length_x, length_y, length_z, waves, cells = sizes
    groups, _, width = atoms_ref.shape
    modes = waves * KZW
    start = wave_start() * waves
    modes_y = start + lax.broadcasted_iota(jnp.int32, (waves, 128), 0)
    modes_z = 1 + lax.broadcasted_iota(jnp.int32, (KZW, 128), 0)
    anchor = lax.axis_index("dx") * MB

    turned = split_dot(forward_ref[...], sums_ref[...])
    cosine = turned[:length_x]
    sine = turned[length_x:]

    green = green_ref[...]
    scaled = jnp.concatenate(
        [
            green * (cosine[:, :modes] + sine[:, modes:]),
            green * (cosine[:, modes:] - sine[:, :modes]),
        ],
        axis=1,
    )
    turned = split_dot(lines_ref[...], scaled)
    cosine = turned[:cells]
    sine = turned[cells:]
    back = jnp.concatenate(
        [cosine[:, :modes] - sine[:, modes:], sine[:, :modes] + cosine[:, modes:]], axis=1
    )
    back_high, back_low = halves(back)
    spare = jnp.zeros((128 - 3 * cells, 2 * modes), jnp.float32)
    stacked = jnp.concatenate([back_high, back_high, back_low, spare], axis=0)
    stacked = jnp.transpose(stacked).astype(jnp.bfloat16)

    for group in range(groups):
        chunk = atoms_ref[group]
        base = chunk[1:4].astype(jnp.int32)
        weights, slopes = spline_rows(chunk[4:7])
        row = lambda d: [w[d : d + 1] for w in weights]
        tilt = lambda d: [w[d : d + 1] for w in slopes]
        factors_y = wave_factors(modes_y, base[1:2], length_y)
        factors_z = wave_factors(modes_z, base[2:3], length_z)
        y_re, y_im = wave_of(factors_y, row(1))
        dy_re, dy_im = wave_of(factors_y, tilt(1))
        z_re, z_im = wave_of(factors_z, row(2))
        dz_re, dz_im = wave_of(factors_z, tilt(2))

        def on_atoms(coeff):
            high, low = halves(cell_rows(coeff, base[0:1] - anchor, cells))
            none = jnp.zeros((128 - 3 * cells, width), jnp.float32)
            right = jnp.concatenate([high, low, high, none], axis=0).astype(jnp.bfloat16)
            return jnp.dot(stacked, right, preferred_element_type=jnp.float32)

        value = on_atoms(row(0))
        slant = on_atoms(tilt(0))

        def along(field, wave_re, wave_im):
            sum_re = jnp.zeros((KZW, width), jnp.float32)
            sum_im = jnp.zeros((KZW, width), jnp.float32)
            for k in range(waves):
                f_re = field[k * KZW : (k + 1) * KZW]
                f_im = field[modes + k * KZW : modes + (k + 1) * KZW]
                k_re = wave_re[k : k + 1]
                k_im = wave_im[k : k + 1]
                sum_re = sum_re + (f_re * k_re - f_im * k_im)
                sum_im = sum_im + (f_re * k_im + f_im * k_re)
            return sum_re, sum_im

        def ended(pair, wave_re, wave_im):
            return 2.0 * jnp.sum(pair[0] * wave_re - pair[1] * wave_im, axis=0, keepdims=True)

        push_x = ended(along(slant, y_re, y_im), z_re, z_im)
        push_y = ended(along(value, dy_re, dy_im), z_re, z_im)
        push_z = ended(along(value, y_re, y_im), dz_re, dz_im)
        force_ref[group] = jnp.concatenate([push_x, push_y, push_z], axis=0) * (
            -chunk[0:1] / cell_size
        )


def long_range(packed, counts):
    count_x = lax.axis_size("dx")
    count_y = lax.axis_size("dy")
    count_z = lax.axis_size("dz")
    groups, _, atom_total = packed.shape
    cells = -(-(MB + 3) // 8) * 8
    length_x = MB * count_x
    length_y = MB * count_y
    length_z = MB * count_z
    waves = MB // count_z
    modes = waves * KZW
    atoms = lax.all_to_all(packed, ("dy", "dz"), 0, 0, tiled=True)
    sums = pl.pallas_call(
        functools.partial(spread_kernel, (length_y, length_z, waves, cells)),
        out_shape=jax.ShapeDtypeStruct((count_x, cells, 2 * modes), jnp.float32),
        compiler_params=pltpu.CompilerParams(vmem_limit_bytes=8 << 20),
    )(atoms)
    received = lax.all_to_all(sums, "dx", 0, 0, tiled=True)
    received = received.reshape(count_x * cells, 2 * modes)
    tables = pl.pallas_call(
        functools.partial(mesh_tables_kernel, (length_x, length_y, length_z, waves, cells)),
        out_shape=[
            jax.ShapeDtypeStruct((2 * length_x, count_x * cells), jnp.float32),
            jax.ShapeDtypeStruct((2 * cells, length_x), jnp.float32),
            jax.ShapeDtypeStruct((length_x, modes), jnp.float32),
        ],
        compiler_params=pltpu.CompilerParams(vmem_limit_bytes=4 << 20),
    )()
    received, counts, tables = lax.optimization_barrier((received, counts, tables))
    parts = pl.pallas_call(
        functools.partial(push_kernel, (length_x, length_y, length_z, waves, cells)),
        out_shape=jax.ShapeDtypeStruct((groups, 3, atom_total), jnp.float32),
        compiler_params=pltpu.CompilerParams(vmem_limit_bytes=16 << 20),
    )(atoms, received, *tables)
    parts = lax.all_to_all(parts, ("dy", "dz"), 0, 0, tiled=True)
    return jnp.sum(parts, axis=0), counts


def shards(
    node_state,
    mesh_base,
    mesh_frac,
    charge,
    nbr_code,
    nbr_count,
    radial_weight,
    mix_weight,
    force_weight,
):
    octants = node_state.shape[3]
    packed, block, own_rows, channel_rows = pack_atoms(
        node_state, mesh_base, mesh_frac, charge, nbr_count, radial_weight, force_weight
    )
    earlier = list_counts(nbr_code, own_rows, 0, 2, ())
    counts, chosen = list_counts(nbr_code, own_rows, 2, 6, earlier)
    long_force, counts = long_range(packed, counts)
    packed_halo = spread_halo(block)
    updated, short_force = neighbour_sums(
        packed_halo, counts, chosen, own_rows, channel_rows, mix_weight
    )
    node_next = updated.reshape(node_state.shape)
    forces = (short_force + long_force).reshape(3, 2, 2, 2, octants)
    return (node_next, forces)


def solution(mesh):
    placed = (
        P("dx", "dy", "dz", None, None),
        P(None, "dx", "dy", "dz", None),
        P(None, "dx", "dy", "dz", None),
        P("dx", "dy", "dz", None),
        P("dx", "dy", "dz", None, None),
        P("dx", "dy", "dz", None),
        P(),
        P(),
        P(),
    )

    return jax.shard_map(
        shards,
        mesh=mesh,
        in_specs=placed,
        out_specs=(P("dx", "dy", "dz", None, None), P(None, "dx", "dy", "dz", None)),
        check_vma=False,
    )
```
